32 devices in a mesh: node: 4 (over x, core), src: 8 (over z, y).
Axes of the slice: x: 2, y: 2, z: 4, core: 2. Of those that a mesh axis runs over, the one named last changes fastest.
Arguments:
- transfer: bfloat16 [306, 61440], P(None, 'node'), may hold values from -0.0234375 to 0.0234375
- node_pos: float32 [3, 61440], P(None, 'node'), may hold values from -1 to 1
- node_layer: int32 [61440], P('node'), may hold values from 0 to 2
- layer_cond: float32 [3], replicated, may hold values from 0.3 to 3
- tile_center: float32 [3, 64], replicated, may hold values from -0.6 to 0.6
- dip_tile: int32 [2048], P('src'), may hold values from 0 to 63
- dip_offset: float32 [3, 2048], P(None, 'src'), may hold values from -0.25 to 0.25
- recording: bfloat16 [306, 12288], P(None, ('node', 'src')), may hold values from -165 to 165, as said below
Outputs:
- sources: bfloat16 [3, 2048, 12288], P(None, 'src', 'node')
The draws below stay inside these ranges and needn't reach their ends.
Inputs may be any that keep to these rules, and one draw needn't show every extreme that they name: `recording`: each sensor has its own gain and offset; the draws stay within the range.
All inputs are finite; a program needn't handle non-finite values.
Results may differ from the reference program's by a relative error of at most 0.0078.
Values may be sent and summed in bfloat16 or wider, within the bound.
A program may use at most 128 MiB of HBM per device.

```python
import math
import jax
import jax.numpy as jnp
from jax import lax

M = 306
NN = 61440
NLAYER = 3
NTILE = 64
NDIP = 2048
TIME = 12288


def draw_recording(key, part):
    key_gain, key_offset, key_noise = jax.random.split(jax.random.fold_in(key, 17), 3)
    sensor_gain = jnp.exp(jax.random.uniform(key_gain, (M, 1), minval=0.0, maxval=math.log(10.0)))
    sensor_offset = jax.random.uniform(key_offset, (M, 1), minval=-1.5, maxval=1.5)
    envelope = 1.0 + 2.0 * jnp.arange(TIME, dtype=jnp.float32)[None, :] / TIME
    noise = jnp.clip(jax.random.normal(key_noise, (M, TIME)), -4.0, 4.0)
    return (sensor_gain * (sensor_offset + noise) * envelope).astype(jnp.bfloat16)


def plant(values, stream_key, least, top_value):
    longest = values.shape.index(max(values.shape))
    spots = []
    for shift in (0, 1):
        where = [jax.random.randint(jax.random.fold_in(stream_key, axis), (), 0, length) for axis, length in enumerate(values.shape)]
        where[longest] = (where[longest] + shift) % values.shape[longest]
        spots.append(tuple(where))
    return values.at[spots[0]].set(least).at[spots[1]].set(top_value)


def steps_of(key, shape, shards, smallest, top_value):
    loudness, own = 1.0, jax.random.fold_in(key, 6)
    for axis_at, shards_of in shards:
        steps = jnp.exp(jax.random.uniform(jax.random.fold_in(own, axis_at), (shards_of,), jnp.float32, smallest / len(shards), top_value / len(shards)))
        loudness = loudness * jnp.repeat(steps, shape[axis_at] // shards_of).reshape([-1 if axis == axis_at else 1 for axis in range(len(shape))])
    return loudness


def normal_values(rng, shape, spread, limit, cuts=(), held_as=jnp.bfloat16):
    factor_of = steps_of(rng, shape, cuts, -0.22, 0.18) if cuts else 1.0
    drawn = jax.random.normal(rng, shape, jnp.float32) * spread * factor_of
    return jnp.minimum(jnp.maximum(drawn, -limit), limit).astype(held_as)


def setup_inputs(seed: int = 0) -> dict:
    streams_of = jax.random.split(jax.random.key(seed), 9)
    return {
        "transfer": normal_values(streams_of[0], (M, NN), NN ** -0.5, 0.0234375, ((1, 4),)),
        "node_pos": jnp.clip(jax.random.uniform(streams_of[1], (3, NN), jnp.float32, -1.0, 1.0) * steps_of(streams_of[1], (3, NN), ((1, 4),), -0.4, 0.0), -1.0, 1.0),
        "node_layer": plant(jax.random.randint(streams_of[2], (NN,), 0, NLAYER), jax.random.fold_in(streams_of[2], 1), 0, NLAYER - 1).astype(jnp.int32),
        "layer_cond": jnp.clip(jnp.exp(jax.random.uniform(streams_of[3], (NLAYER,), jnp.float32, math.log(0.3), math.log(3.0))), 0.3, 3.0),
        "tile_center": jnp.clip(jax.random.uniform(streams_of[4], (3, NTILE), jnp.float32, -0.6, 0.6), -0.6, 0.6),
        "dip_tile": plant(jax.random.randint(streams_of[5], (NDIP,), 0, NTILE), jax.random.fold_in(streams_of[5], 1), 0, NTILE - 1).astype(jnp.int32),
        "dip_offset": normal_values(streams_of[6], (3, NDIP), 0.05, 0.25, ((1, 8),), jnp.float32),
        "recording": draw_recording(jax.random.fold_in(streams_of[8], 71), 0),
    }


SOFTENING = 0.02
COV_RIDGE = 0.05
GRAM_RIDGE = 0.01
EPSILON = 1e-06

def place_dipoles(tile_center, dip_tile, dip_offset):
    tile_ids = jnp.arange(tile_center.shape[1], dtype=jnp.int32)
    onehot = (tile_ids[:, None] == dip_tile[None, :]).astype(jnp.float32)
    return jnp.dot(tile_center, onehot, precision=lax.Precision.HIGHEST) + dip_offset

def layer_scale(node_layer, layer_cond):
    levels = jnp.arange(layer_cond.shape[0], dtype=jnp.int32)
    onehot = (node_layer[None, :] == levels[:, None]).astype(jnp.float32)
    return lax.optimization_barrier(jnp.sum(layer_cond[:, None] * onehot, axis=0))

def potential_block(node_block, scales, dip_pos):
    offsets = node_block[:, :, None] - dip_pos[:, None, :]
    squared = lax.optimization_barrier(jnp.sum(offsets * offsets, axis=0)) + SOFTENING
    weights = scales[:, None] / (squared * jnp.sqrt(squared))
    return jnp.concatenate([offsets[0] * weights, offsets[1] * weights, offsets[2] * weights], axis=1).astype(jnp.bfloat16)

def lead_partial(transfer, node_pos, scales, dip_pos):
    node_rows = transfer.shape[1]
    block_rows = math.gcd(node_rows, 3072)

    def advance(carry, position):
        first_row = position * block_rows
        node_block = lax.dynamic_slice_in_dim(node_pos, first_row, block_rows, 1)
        scale_block = lax.dynamic_slice_in_dim(scales, first_row, block_rows, 0)
        transfer_block = lax.dynamic_slice_in_dim(transfer, first_row, block_rows, 1)
        potential = potential_block(node_block, scale_block, dip_pos)
        return (carry + jnp.dot(transfer_block.astype(jnp.float32), potential.astype(jnp.float32), preferred_element_type=jnp.float32), None)
    start_value = jnp.zeros((transfer.shape[0], 3 * dip_pos.shape[1]), jnp.float32)
    result, _ = lax.scan(advance, start_value, jnp.arange(node_rows // block_rows, dtype=jnp.int32))
    return result

def invert_three(matrix):

    def entry(row_index, col_index):
        return matrix[row_index % 3, col_index % 3]
    cofactor = [[entry(row_index + 1, col_index + 1) * entry(row_index + 2, col_index + 2) - entry(row_index + 1, col_index + 2) * entry(row_index + 2, col_index + 1) for col_index in range(3)] for row_index in range(3)]
    determinant = matrix[0, 0] * cofactor[0][0] + matrix[0, 1] * cofactor[0][1] + matrix[0, 2] * cofactor[0][2]
    return jnp.stack([jnp.stack([cofactor[col_index][row_index] / determinant for col_index in range(3)]) for row_index in range(3)])

def make_filters(leadfield, cross_sum, sample_sum, sample_count):
    sensors = leadfield.shape[0]
    mean_square = lax.optimization_barrier(jnp.mean(leadfield * leadfield, axis=(0, 1)))
    normed = leadfield / jnp.sqrt(mean_square + EPSILON)[None, None, :]
    average = sample_sum / sample_count
    covariance = (cross_sum - sample_count * jnp.outer(average, average)) / (sample_count - 1.0)
    covariance = covariance + COV_RIDGE * jnp.trace(covariance) / sensors * jnp.eye(sensors, dtype=jnp.float32)
    factor = jnp.linalg.cholesky(covariance)
    flat = normed.reshape(sensors, -1)
    middle = lax.linalg.triangular_solve(factor, flat, left_side=True, lower=True)
    solved = lax.linalg.triangular_solve(factor, middle, left_side=True, lower=True, transpose_a=True)
    solved = solved.reshape(normed.shape)
    gram_matrix = jnp.einsum('mcj,mdj->cdj', normed, solved, precision=lax.Precision.HIGHEST)
    ridge_term = GRAM_RIDGE * (gram_matrix[0, 0] + gram_matrix[1, 1] + gram_matrix[2, 2]) / 3.0
    gram_matrix = gram_matrix + ridge_term[None, None, :] * jnp.eye(3, dtype=jnp.float32)[:, :, None]
    inverse = invert_three(gram_matrix)
    filters = jnp.einsum('cdj,mdj->mcj', inverse, solved, precision=lax.Precision.HIGHEST)
    return filters.astype(jnp.bfloat16)

def reference(transfer, node_pos, node_layer, layer_cond, tile_center, dip_tile, dip_offset, recording):
    dip_pos = place_dipoles(tile_center, dip_tile, dip_offset)
    scales = layer_scale(node_layer, layer_cond)
    leadfield = lead_partial(transfer, node_pos, scales, dip_pos).reshape(M, 3, NDIP)
    cross_sum = jnp.dot(recording.astype(jnp.float32), recording.T.astype(jnp.float32), preferred_element_type=jnp.float32)
    sample_sum = lax.optimization_barrier(jnp.sum(recording.astype(jnp.float32), axis=1))
    filters = make_filters(leadfield, cross_sum, sample_sum, float(TIME))
    courses = []
    for component in range(3):
        courses.append(jnp.dot(filters[:, component, :].T.astype(jnp.float32), recording.astype(jnp.float32), preferred_element_type=jnp.float32).astype(jnp.bfloat16))
    return jnp.stack(courses)
```

```python
import functools
import math

import jax
import jax.numpy as jnp
from jax import lax
from jax.experimental import pallas as pl
from jax.experimental.pallas import tpu as pltpu
from jax.sharding import PartitionSpec as P

SOFTENING = 0.02
COV_RIDGE = 0.05
GRAM_RIDGE = 0.01
EPSILON = 1e-06
NT = (((1,), (1,)), ((), ()))
F32 = jnp.float32
BF16 = jnp.bfloat16


def round_up(value, unit):
    return -(-value // unit) * unit


def place_dipoles(tile_center, dip_tile, dip_offset):
    tile_ids = jnp.arange(tile_center.shape[1], dtype=jnp.int32)
    onehot = (tile_ids[:, None] == dip_tile[None, :]).astype(F32)
    return jnp.dot(tile_center, onehot, precision=lax.Precision.HIGHEST) + dip_offset


def layer_scale(node_layer, layer_cond):
    levels = jnp.arange(layer_cond.shape[0], dtype=jnp.int32)
    onehot = (node_layer[None, :] == levels[:, None]).astype(F32)
    return jnp.sum(layer_cond[:, None] * onehot, axis=0)


def remote(held, dst, send_sem, recv_sem, **where):
    return pltpu.make_async_remote_copy(
        src_ref=held, dst_ref=dst, send_sem=send_sem, recv_sem=recv_sem,
        device_id=where, device_id_type=pl.DeviceIdType.MESH,
    )


def potential_rows(node, dip, rows):
    dipoles = dip.shape[0]
    parts = [[], [], []]
    for first in range(0, dipoles, rows):
        offsets = [node[c : c + 1, :] - dip[first : first + rows, c : c + 1] for c in range(3)]
        q = offsets[0] * offsets[0] + offsets[1] * offsets[1] + offsets[2] * offsets[2] + SOFTENING
        root = lax.rsqrt(q)
        weights = (node[3:4, :] * root) * (root * root)
        for c in range(3):
            parts[c].append((offsets[c] * weights).astype(BF16))
    return jnp.concatenate(parts[0] + parts[1] + parts[2], axis=0)


def lead_kernel(
    nd, ns, r, stages,
    rec, transfer, node, dip, cross_out, lead_out,
    aug, acc, buf, got_a, part, got_b, fin, res,
    s_a, r_a, s_b, r_b, s_c, r_c, s_d, r_d,
):
    step = pl.program_id(0)
    me_n, me_s = lax.axis_index("node"), lax.axis_index("src")
    sensors = rec.shape[0]
    dipoles = dip.shape[0]
    mp = aug.shape[0]
    peer_n = [None] + [lax.rem(me_n + k, nd) for k in range(1, nd)]
    peer_s = [None] + [lax.rem(me_s + k, ns) for k in range(1, ns)]

    def copy_a(k):
        return remote(buf.at[peer_n[k]], got_a.at[k - 1], s_a.at[k - 1], r_a.at[k - 1], node=peer_n[k])

    def copy_b(k):
        return remote(part.at[peer_s[k]], got_b.at[k - 1], s_b.at[k - 1], r_b.at[k - 1], src=peer_s[k])

    def copy_c(k):
        return remote(fin, res.at[me_n, me_s], s_c.at[k - 1], r_c.at[k - 1], src=peer_s[k])

    def copy_d(k):
        return remote(res.at[me_n], res.at[me_n], s_d.at[k - 1], r_d.at[k - 1], node=peer_n[k])

    @pl.when(step == stages[0])
    def _():
        barrier = pltpu.get_barrier_semaphore()
        for k in range(1, nd):
            pl.semaphore_signal(barrier, inc=1, device_id={"node": peer_n[k]}, device_id_type=pl.DeviceIdType.MESH)
        for k in range(1, ns):
            pl.semaphore_signal(barrier, inc=1, device_id={"src": peer_s[k]}, device_id_type=pl.DeviceIdType.MESH)
        acc[...] = jnp.zeros_like(acc)
        low = sensors // 16 * 16
        tail = lax.broadcasted_iota(jnp.int32, (mp - low, aug.shape[1]), 0) + low
        aug[low:, :] = jnp.where(tail == sensors, 1.0, 0.0).astype(BF16)
        aug[:sensors, :] = rec[...]
        held = aug[...]
        cross = lax.dot_general(held, held, NT, preferred_element_type=F32)
        for n in range(nd):
            for s in range(ns):
                first = (n * ns + s) * r
                buf[n, s] = cross[first : first + r, :]
        pl.semaphore_wait(barrier, nd - 1 + ns - 1)

    @pl.when(step == stages[1])
    def _():
        for k in range(1, nd):
            copy_a(k).start()

    @pl.when(step == stages[2])
    def _():
        total = buf[me_n]
        for k in range(1, nd):
            copy_a(k).wait()
            total = total + got_a[k - 1]
        part[...] = total

    @pl.when(step == stages[3])
    def _():
        for k in range(1, ns):
            copy_b(k).start()

    @pl.when(step == stages[4])
    def _():
        total = part[me_s]
        for k in range(1, ns):
            copy_b(k).wait()
            total = total + got_b[k - 1]
        fin[...] = total
        res[me_n, me_s] = total

    @pl.when(step == stages[5])
    def _():
        for k in range(1, ns):
            copy_c(k).start()

    @pl.when(step == stages[6])
    def _():
        for k in range(1, ns):
            copy_c(k).wait()
        for k in range(1, nd):
            copy_d(k).start()

    block = transfer.shape[1]
    sub = math.gcd(block, 512)
    dip_now = dip[...]
    total = None
    for first in range(0, block, sub):
        potential = potential_rows(node[:, first : first + sub], dip_now, 32)
        product = lax.dot_general(
            transfer[:, first : first + sub], potential, NT, preferred_element_type=F32
        )
        total = product if total is None else total + product
    acc[:sensors, :] += total

    @pl.when(step == stages[7])
    def _():
        flipped = acc[...].T
        own = dipoles // nd
        for n in range(nd):
            for c in range(3):
                first = c * dipoles + n * own
                lead_out[n, c] = flipped[first : first + own, :]
        for k in range(1, nd):
            copy_d(k).wait()
        cross_out[...] = jnp.zeros_like(cross_out)
        for n in range(nd):
            for s in range(ns):
                first = (n * ns + s) * r
                cross_out[first : first + r, :] = res[n, s]


def lead_and_cross(rec, transfer, node, dip):
    nd, ns = lax.axis_size("node"), lax.axis_size("src")
    sensors, time = rec.shape
    nodes = transfer.shape[1]
    dipoles = dip.shape[0]
    mp = round_up(sensors + 1, 128)
    r = -(-(sensors + 1) // (nd * ns))
    block = math.gcd(nodes, 1024)
    steps = nodes // block
    last = steps - 1
    stages = (0, 1, last * 4 // 14, last * 5 // 14, last * 8 // 14, last * 9 // 14, last * 12 // 14, last)
    chunk = (nd, ns, r, mp)
    vmem = pl.BlockSpec(memory_space=pltpu.VMEM)
    return pl.pallas_call(
        functools.partial(lead_kernel, nd, ns, r, stages),
        grid=(steps,),
        out_shape=(
            jax.ShapeDtypeStruct((mp, mp), F32),
            jax.ShapeDtypeStruct((nd, 3, dipoles // nd, mp), F32),
        ),
        in_specs=[
            vmem,
            pl.BlockSpec((sensors, block), lambda i: (0, i)),
            pl.BlockSpec((4, block), lambda i: (0, i)),
            vmem,
        ],
        out_specs=(vmem, vmem),
        scratch_shapes=[
            pltpu.VMEM((mp, time), BF16),
            pltpu.VMEM((mp, 3 * dipoles), F32),
            pltpu.VMEM(chunk, F32),
            pltpu.VMEM((nd - 1,) + chunk[1:], F32),
            pltpu.VMEM(chunk[1:], F32),
            pltpu.VMEM((ns - 1,) + chunk[2:], F32),
            pltpu.VMEM(chunk[2:], F32),
            pltpu.VMEM(chunk, F32),
        ]
        + [pltpu.SemaphoreType.DMA((n,)) for n in (nd - 1, nd - 1, ns - 1, ns - 1, ns - 1, ns - 1, nd - 1, nd - 1)],
        compiler_params=pltpu.CompilerParams(collective_id=0, has_side_effects=True),
        name="lead_cross",
    )(rec, transfer, node, dip)


def dot_full(a, b):
    return jnp.dot(a, b, precision=lax.Precision.HIGHEST, preferred_element_type=F32)


def halves(a):
    high = a.astype(BF16)
    return high, (a - high.astype(F32)).astype(BF16)


def dot_three(a, b):
    (ah, al), (bh, bl) = a, b
    dot = functools.partial(jnp.dot, preferred_element_type=F32)
    return dot(ah, bh) + (dot(ah, bl) + dot(al, bh))


def covariance_inverse(cross, sensors, count, full_steps):
    mp = cross.shape[0]
    rows = lax.broadcasted_iota(jnp.int32, (mp, mp), 0)
    cols = lax.broadcasted_iota(jnp.int32, (mp, mp), 1)
    average = cross[:, sensors : sensors + 1] / count
    sums = cross[sensors : sensors + 1, :]
    cov = (cross - average * sums) / (count - 1.0)
    cov = jnp.where((rows < sensors) & (cols < sensors), cov, 0.0)
    diagonal = rows == cols
    trace = jnp.sum(jnp.sum(jnp.where(diagonal, cov, 0.0), axis=1, keepdims=True), axis=0, keepdims=True)
    ridge = COV_RIDGE / sensors * trace
    centre = 0.5 * trace + ridge
    scaled = cov / centre + jnp.where(diagonal, jnp.where(rows < sensors, ridge / centre, 1.0), 0.0)
    ratio = sensors / COV_RIDGE + 1.0
    h = (ratio - 1.0) / (ratio + 1.0)
    plan = []
    while h > 1e-5:
        plan.append(1.0 / (2.0 - h * h))
        h = h * h / (2.0 - h * h)
    eye = jnp.where(diagonal, 1.0, 0.0)
    x = (4.0 * plan[0]) * eye - (2.0 * plan[0]) * scaled
    scaled_halves = halves(scaled)
    for at, gain in enumerate(plan[1:], 1):
        if at >= len(plan) - full_steps:
            y = dot_full(scaled, x)
            x = dot_full(x, (4.0 * gain) * eye - (2.0 * gain) * y)
        else:
            xh = halves(x)
            y = dot_three(scaled_halves, xh)
            x = dot_three(xh, halves((4.0 * gain) * eye - (2.0 * gain) * y))
    return x / centre


def filter_kernel(
    nd, ns, inner, count,
    cross, lead, rec, filt, rec_all,
    got, s_l, r_l, s_y, r_y, s_z, r_z, s_f, r_f,
):
    me_n, me_s = lax.axis_index("node"), lax.axis_index("src")
    outer = ns // inner
    sensors, time = rec.shape
    own = lead.shape[2]
    mp = cross.shape[0]
    hi, lo = me_s // inner, lax.rem(me_s, inner)
    peer_n = [None] + [lax.rem(me_n + k, nd) for k in range(1, nd)]
    peer_z = [None] + [lax.rem(hi + k, outer) * inner + lo for k in range(1, outer)]
    from_z = [me_s] + [lax.rem(hi + outer - k, outer) * inner + lo for k in range(1, outer)]
    peer_y = hi * inner + lax.rem(lo + 1, inner)

    def columns(s):
        return rec_all.at[:, pl.ds(pl.multiple_of(s * time, time), time)]

    def copy_l(k):
        return remote(lead.at[peer_n[k]], got.at[k - 1], s_l.at[k - 1], r_l.at[k - 1], node=peer_n[k])

    def copy_y(k):
        source = rec if k == 0 else columns(from_z[k])
        return remote(source, columns(from_z[k]), s_y.at[k], r_y.at[k], src=peer_y)

    def copy_z(k):
        return remote(rec, columns(me_s), s_z.at[k - 1], r_z.at[k - 1], src=peer_z[k])

    def copy_f(k):
        return remote(filt.at[:, me_n], filt.at[:, me_n], s_f.at[k - 1], r_f.at[k - 1], node=peer_n[k])

    barrier = pltpu.get_barrier_semaphore()
    for k in range(1, nd):
        pl.semaphore_signal(barrier, inc=1, device_id={"node": peer_n[k]}, device_id_type=pl.DeviceIdType.MESH)
    for k in range(1, outer):
        pl.semaphore_signal(barrier, inc=1, device_id={"src": peer_z[k]}, device_id_type=pl.DeviceIdType.MESH)
    pl.semaphore_signal(barrier, inc=1, device_id={"src": peer_y}, device_id_type=pl.DeviceIdType.MESH)
    pl.semaphore_wait(barrier, nd - 1 + outer)

    for k in range(1, nd):
        copy_l(k).start()
    copy_y(0).start()
    for k in range(1, outer):
        copy_z(k).start()
    rec_all[:, pl.ds(pl.multiple_of(me_s * time, time), time)] = rec[...]

    inverse = covariance_inverse(cross[...], sensors, count, 3)

    for k in range(1, outer):
        copy_z(k).wait()
        copy_y(k).start()
    field = lead[me_n]
    for k in range(1, nd):
        copy_l(k).wait()
        field = field + got[k - 1]
    square = jnp.sum(jnp.sum(field * field, axis=0), axis=1, keepdims=True) / (3.0 * sensors)
    normed = field / jnp.sqrt(square + EPSILON)[None]
    solved = dot_full(normed.reshape(3 * own, mp), inverse).reshape(3, own, mp)
    gram = {}
    for c in range(3):
        for d in range(c, 3):
            gram[c, d] = jnp.sum(normed[c] * solved[d], axis=1, keepdims=True)
            gram[d, c] = gram[c, d]
    ridge = GRAM_RIDGE * (gram[0, 0] + gram[1, 1] + gram[2, 2]) / 3.0
    for c in range(3):
        gram[c, c] = gram[c, c] + ridge

    def cofactor(row, col):
        a, b, c, d = (row + 1) % 3, (row + 2) % 3, (col + 1) % 3, (col + 2) % 3
        return gram[a, c] * gram[b, d] - gram[a, d] * gram[b, c]

    determinant = gram[0, 0] * cofactor(0, 0) + gram[0, 1] * cofactor(0, 1) + gram[0, 2] * cofactor(0, 2)
    for c in range(3):
        mixed = sum((cofactor(d, c) / determinant) * solved[d] for d in range(3))
        filt[c, me_n] = mixed[:, :sensors].astype(BF16)
    for k in range(1, nd):
        copy_f(k).start()
    for k in range(outer):
        copy_y(k).wait()
    for k in range(1, nd):
        copy_f(k).wait()


def make_filters(cross, lead, rec):
    nd, ns = lax.axis_size("node"), lax.axis_size("src")
    sensors, time = rec.shape
    own, mp = lead.shape[2:]
    inner = 2
    outer = ns // inner
    vmem = pl.BlockSpec(memory_space=pltpu.VMEM)
    return pl.pallas_call(
        functools.partial(filter_kernel, nd, ns, inner, float(time * nd * ns)),
        out_shape=(
            jax.ShapeDtypeStruct((3, nd, own, sensors), BF16),
            jax.ShapeDtypeStruct((sensors, ns * time), BF16),
        ),
        in_specs=[vmem] * 3,
        out_specs=(vmem, vmem),
        scratch_shapes=[pltpu.VMEM((nd - 1,) + lead.shape[1:], F32)]
        + [pltpu.SemaphoreType.DMA((n,)) for n in (nd - 1, nd - 1, outer, outer, outer - 1, outer - 1, nd - 1, nd - 1)],
        compiler_params=pltpu.CompilerParams(collective_id=1, has_side_effects=True),
        name="filters",
    )(cross, lead, rec)


def local(transfer, node_pos, node_layer, layer_cond, tile_center, dip_tile, dip_offset, recording):
    sensors = transfer.shape[0]
    dipoles = dip_tile.shape[0]
    dip_pos = place_dipoles(tile_center, dip_tile, dip_offset)
    scales = layer_scale(node_layer, layer_cond)
    node = jnp.concatenate([node_pos, scales[None, :]], axis=0)
    cross, lead = lead_and_cross(recording, transfer, node, dip_pos.T)
    filters, samples = make_filters(cross, lead, recording)
    out = jnp.dot(filters.reshape(3 * dipoles, sensors), samples, preferred_element_type=F32)
    return out.astype(BF16).reshape(3, dipoles, samples.shape[1])


def solution(mesh):
    return jax.shard_map(
        local,
        mesh=mesh,
        in_specs=(
            P(None, "node"),
            P(None, "node"),
            P("node"),
            P(),
            P(),
            P("src"),
            P(None, "src"),
            P(None, ("node", "src")),
        ),
        out_specs=P(None, "src", "node"),
        check_vma=False,
    )
```

```python
import functools
import math

import jax
import jax.numpy as jnp
from jax import lax
from jax.experimental import pallas as pl
from jax.experimental.pallas import tpu as pltpu
from jax.sharding import PartitionSpec as P

SOFTENING = 0.02
COV_RIDGE = 0.05
GRAM_RIDGE = 0.01
EPSILON = 1e-06
NT = (((1,), (1,)), ((), ()))
F32 = jnp.float32
BF16 = jnp.bfloat16


def round_up(value, unit):
    return -(-value // unit) * unit


def place_dipoles(tile_center, dip_tile, dip_offset):
    tiles, dipoles = tile_center.shape[1], dip_tile.shape[1]
    onehot = (lax.broadcasted_iota(jnp.int32, (tiles, dipoles), 0) == dip_tile).astype(F32)
    rows = jnp.dot(tile_center, onehot, precision=lax.Precision.HIGHEST, preferred_element_type=F32) + dip_offset
    return jnp.concatenate([rows, jnp.zeros((128 - rows.shape[0], dipoles), F32)], axis=0).T


def layer_scale(node_layer, layer_cond):
    scale = jnp.zeros(node_layer.shape, F32)
    for level in range(layer_cond.shape[0]):
        scale = jnp.where(node_layer == level, layer_cond[level], scale)
    return scale


def remote(held, dst, send_sem, recv_sem, **where):
    return pltpu.make_async_remote_copy(
        src_ref=held, dst_ref=dst, send_sem=send_sem, recv_sem=recv_sem,
        device_id=where, device_id_type=pl.DeviceIdType.MESH,
    )


def potential_rows(node, scale, dip, rows):
    dipoles = dip.shape[0]
    parts = [[], [], []]
    for first in range(0, dipoles, rows):
        offsets = [node[c : c + 1, :] - dip[first : first + rows, c : c + 1] for c in range(3)]
        q = offsets[0] * offsets[0] + offsets[1] * offsets[1] + offsets[2] * offsets[2] + SOFTENING
        root = lax.rsqrt(q)
        weights = (scale * root) * (root * root)
        for c in range(3):
            parts[c].append((offsets[c] * weights).astype(BF16))
    return jnp.concatenate(parts[0] + parts[1] + parts[2], axis=0)


def lead_kernel(
    nd, ns, inner, r, stages,
    rec, transfer, node, layer, cond, centre, tile, offset, cross_out, lead_out, z_out,
    dip, aug, acc, buf, got_a, part, got_b, fin, res,
    s_a, r_a, s_b, r_b, s_c, r_c, s_d, r_d, s_z, r_z, own_sem,
):
    step = pl.program_id(0)
    me_n, me_s = lax.axis_index("node"), lax.axis_index("src")
    sensors = rec.shape[0]
    dipoles = dip.shape[0]
    mp = aug.shape[0]
    outer = ns // inner
    hi, lo = me_s // inner, lax.rem(me_s, inner)
    peer_n = [None] + [lax.rem(me_n + k, nd) for k in range(1, nd)]
    peer_s = [None] + [lax.rem(me_s + k, ns) for k in range(1, ns)]

    def copy_a(k):
        return remote(buf.at[peer_n[k]], got_a.at[k - 1], s_a.at[k - 1], r_a.at[k - 1], node=peer_n[k])

    def copy_b(k):
        return remote(part.at[peer_s[k]], got_b.at[k - 1], s_b.at[k - 1], r_b.at[k - 1], src=peer_s[k])

    def copy_c(k):
        return remote(fin, res.at[me_n, me_s], s_c.at[k - 1], r_c.at[k - 1], src=peer_s[k])

    def copy_d(k):
        return remote(res.at[me_n], res.at[me_n], s_d.at[k - 1], r_d.at[k - 1], node=peer_n[k])

    def copy_z(k):
        peer = lax.rem(hi + k, outer) * inner + lo
        return remote(rec, z_out.at[hi], s_z.at[k - 1], r_z.at[k - 1], src=peer)

    keep = pltpu.make_async_copy(rec, z_out.at[hi], own_sem)

    @pl.when(step == stages[0])
    def _():
        barrier = pltpu.get_barrier_semaphore()
        for k in range(1, nd):
            pl.semaphore_signal(barrier, inc=1, device_id={"node": peer_n[k]}, device_id_type=pl.DeviceIdType.MESH)
        for k in range(1, ns):
            pl.semaphore_signal(barrier, inc=1, device_id={"src": peer_s[k]}, device_id_type=pl.DeviceIdType.MESH)
        acc[...] = jnp.zeros_like(acc)
        low = sensors // 16 * 16
        tail = lax.broadcasted_iota(jnp.int32, (mp - low, aug.shape[1]), 0) + low
        aug[low:, :] = jnp.where(tail == sensors, 1.0, 0.0).astype(BF16)
        aug[:sensors, :] = rec[...]
        held = aug[...]
        cross = lax.dot_general(held, held, NT, preferred_element_type=F32)
        for n in range(nd):
            for s in range(ns):
                first = (n * ns + s) * r
                buf[n, s] = cross[first : first + r, :]
        pl.semaphore_wait(barrier, nd - 1 + ns - 1)
        for k in range(1, nd):
            copy_a(k).start()
        keep.start()
        for k in range(1, outer, 2):
            copy_z(k).start()
        dip[...] = place_dipoles(centre[...], tile[...], offset[...])

    @pl.when(step == stages[1])
    def _():
        total = buf[me_n]
        for k in range(1, nd):
            copy_a(k).wait()
            total = total + got_a[k - 1]
        part[...] = total
        for k in range(1, ns):
            copy_b(k).start()

    @pl.when(step == stages[2])
    def _():
        total = part[me_s]
        for k in range(1, ns):
            copy_b(k).wait()
            total = total + got_b[k - 1]
        fin[...] = total
        res[me_n, me_s] = total
        for k in range(1, ns):
            copy_c(k).start()
        for k in range(2, outer, 2):
            copy_z(k).start()

    @pl.when(step == stages[3])
    def _():
        for k in range(1, ns):
            copy_c(k).wait()
        for k in range(1, nd):
            copy_d(k).start()

    block = transfer.shape[1]
    sub = math.gcd(block, 512)
    dip_now = dip[...]
    scale = layer_scale(layer[...], cond)
    total = None
    for first in range(0, block, sub):
        potential = potential_rows(
            node[:, first : first + sub], scale[:, first : first + sub], dip_now, 32
        )
        product = lax.dot_general(
            transfer[:, first : first + sub], potential, NT, preferred_element_type=F32
        )
        total = product if total is None else total + product
    acc[:sensors, :] += total

    @pl.when(step == stages[4])
    def _():
        flipped = acc[...].T
        own = dipoles // nd
        for n in range(nd):
            for c in range(3):
                first = c * dipoles + n * own
                lead_out[n, c] = flipped[first : first + own, :]
        for k in range(1, nd):
            copy_d(k).wait()
        cross_out[...] = jnp.zeros_like(cross_out)
        for n in range(nd):
            for s in range(ns):
                first = (n * ns + s) * r
                cross_out[first : first + r, :] = res[n, s]
        keep.wait()
        for k in range(1, outer):
            copy_z(k).wait()


def lead_and_cross(inner, rec, transfer, node, layer, cond, centre, tile, offset):
    nd, ns = lax.axis_size("node"), lax.axis_size("src")
    sensors, time = rec.shape
    nodes = transfer.shape[1]
    dipoles = tile.shape[1]
    outer = ns // inner
    mp = round_up(sensors + 1, 128)
    r = -(-(sensors + 1) // (nd * ns))
    block = math.gcd(nodes, 1024)
    steps = nodes // block
    last = steps - 1
    stages = (0, last * 4 // 14, last * 8 // 14, last * 11 // 14, last)
    chunk = (nd, ns, r, mp)
    vmem = pl.BlockSpec(memory_space=pltpu.VMEM)
    return pl.pallas_call(
        functools.partial(lead_kernel, nd, ns, inner, r, stages),
        grid=(steps,),
        out_shape=(
            jax.ShapeDtypeStruct((mp, mp), F32),
            jax.ShapeDtypeStruct((nd, 3, dipoles // nd, mp), F32),
            jax.ShapeDtypeStruct((outer, sensors, time), BF16),
        ),
        in_specs=[
            vmem,
            pl.BlockSpec((sensors, block), lambda i: (0, i)),
            pl.BlockSpec((3, block), lambda i: (0, i)),
            pl.BlockSpec((1, block), lambda i: (0, i)),
            pl.BlockSpec(memory_space=pltpu.SMEM),
            vmem,
            vmem,
            vmem,
        ],
        out_specs=(vmem, vmem, pl.BlockSpec(memory_space=pl.ANY)),
        scratch_shapes=[
            pltpu.VMEM((dipoles, 128), F32),
            pltpu.VMEM((mp, time), BF16),
            pltpu.VMEM((mp, 3 * dipoles), F32),
            pltpu.VMEM(chunk, F32),
            pltpu.VMEM((nd - 1,) + chunk[1:], F32),
            pltpu.VMEM(chunk[1:], F32),
            pltpu.VMEM((ns - 1,) + chunk[2:], F32),
            pltpu.VMEM(chunk[2:], F32),
            pltpu.VMEM(chunk, F32),
        ]
        + [pltpu.SemaphoreType.DMA((n,)) for n in (nd - 1, nd - 1, ns - 1, ns - 1, ns - 1, ns - 1, nd - 1, nd - 1, outer - 1, outer - 1)]
        + [pltpu.SemaphoreType.DMA],
        compiler_params=pltpu.CompilerParams(collective_id=0, has_side_effects=True),
        name="lead_cross",
    )(rec, transfer, node, layer, cond, centre, tile, offset)


def dot_full(a, b):
    return jnp.dot(a, b, precision=lax.Precision.HIGHEST, preferred_element_type=F32)


def halves(a):
    high = a.astype(BF16)
    return high, (a - high.astype(F32)).astype(BF16)


def dot_three(a, b):
    (ah, al), (bh, bl) = a, b
    dot = functools.partial(jnp.dot, preferred_element_type=F32)
    return dot(ah, bh) + (dot(ah, bl) + dot(al, bh))


def covariance_inverse(cross, sensors, count, full_steps):
    mp = cross.shape[0]
    rows = lax.broadcasted_iota(jnp.int32, (mp, mp), 0)
    cols = lax.broadcasted_iota(jnp.int32, (mp, mp), 1)
    average = cross[:, sensors : sensors + 1] / count
    sums = cross[sensors : sensors + 1, :]
    cov = (cross - average * sums) / (count - 1.0)
    cov = jnp.where((rows < sensors) & (cols < sensors), cov, 0.0)
    diagonal = rows == cols
    trace = jnp.sum(jnp.sum(jnp.where(diagonal, cov, 0.0), axis=1, keepdims=True), axis=0, keepdims=True)
    ridge = COV_RIDGE / sensors * trace
    centre = 0.5 * trace + ridge
    scaled = cov / centre + jnp.where(diagonal, jnp.where(rows < sensors, ridge / centre, 1.0), 0.0)
    ratio = sensors / COV_RIDGE + 1.0
    h = (ratio - 1.0) / (ratio + 1.0)
    plan = []
    while h > 1e-5:
        plan.append(1.0 / (2.0 - h * h))
        h = h * h / (2.0 - h * h)
    eye = jnp.where(diagonal, 1.0, 0.0)
    x = (4.0 * plan[0]) * eye - (2.0 * plan[0]) * scaled
    scaled_halves = halves(scaled)
    for at, gain in enumerate(plan[1:], 1):
        if at >= len(plan) - full_steps:
            y = dot_full(scaled, x)
            x = dot_full(x, (4.0 * gain) * eye - (2.0 * gain) * y)
        else:
            xh = halves(x)
            y = dot_three(scaled_halves, xh)
            x = dot_three(xh, halves((4.0 * gain) * eye - (2.0 * gain) * y))
    return x / centre


def filter_kernel(
    nd, ns, inner, count,
    cross, lead, held, filt, rec_all,
    got, s_l, r_l, s_y, r_y, s_f, r_f,
):
    me_n, me_s = lax.axis_index("node"), lax.axis_index("src")
    outer = ns // inner
    sensors, time = held.shape[1:]
    own = lead.shape[2]
    mp = cross.shape[0]
    hi, lo = me_s // inner, lax.rem(me_s, inner)
    peer_n = [None] + [lax.rem(me_n + k, nd) for k in range(1, nd)]
    peer_y = hi * inner + lax.rem(lo + 1, inner)

    def columns(s):
        return rec_all.at[:, pl.ds(pl.multiple_of(s * time, time), time)]

    def copy_l(k):
        return remote(lead.at[peer_n[k]], got.at[k - 1], s_l.at[k - 1], r_l.at[k - 1], node=peer_n[k])

    def copy_y(k):
        return remote(held.at[k], columns(k * inner + lo), s_y.at[k], r_y.at[k], src=peer_y)

    def copy_f(k):
        return remote(filt.at[:, me_n], filt.at[:, me_n], s_f.at[k - 1], r_f.at[k - 1], node=peer_n[k])

    barrier = pltpu.get_barrier_semaphore()
    for k in range(1, nd):
        pl.semaphore_signal(barrier, inc=1, device_id={"node": peer_n[k]}, device_id_type=pl.DeviceIdType.MESH)
    pl.semaphore_signal(barrier, inc=1, device_id={"src": peer_y}, device_id_type=pl.DeviceIdType.MESH)
    pl.semaphore_wait(barrier, nd - 1 + 1)

    for k in range(1, nd):
        copy_l(k).start()
    for k in range(outer):
        copy_y(k).start()
    for k in range(outer):
        first = pl.multiple_of((k * inner + lo) * time, time)
        rec_all[:, pl.ds(first, time)] = held[k]

    inverse = covariance_inverse(cross[...], sensors, count, 2)

    field = lead[me_n]
    for k in range(1, nd):
        copy_l(k).wait()
        field = field + got[k - 1]
    square = jnp.sum(jnp.sum(field * field, axis=0), axis=1, keepdims=True) / (3.0 * sensors)
    normed = field / jnp.sqrt(square + EPSILON)[None]
    solved = dot_full(normed.reshape(3 * own, mp), inverse).reshape(3, own, mp)
    gram = {}
    for c in range(3):
        for d in range(c, 3):
            gram[c, d] = jnp.sum(normed[c] * solved[d], axis=1, keepdims=True)
            gram[d, c] = gram[c, d]
    ridge = GRAM_RIDGE * (gram[0, 0] + gram[1, 1] + gram[2, 2]) / 3.0
    for c in range(3):
        gram[c, c] = gram[c, c] + ridge

    def cofactor(row, col):
        a, b, c, d = (row + 1) % 3, (row + 2) % 3, (col + 1) % 3, (col + 2) % 3
        return gram[a, c] * gram[b, d] - gram[a, d] * gram[b, c]

    determinant = gram[0, 0] * cofactor(0, 0) + gram[0, 1] * cofactor(0, 1) + gram[0, 2] * cofactor(0, 2)
    for c in range(3):
        mixed = sum((cofactor(d, c) / determinant) * solved[d] for d in range(3))
        filt[c, me_n] = mixed[:, :sensors].astype(BF16)
    for k in range(1, nd):
        copy_f(k).start()
    for k in range(outer):
        copy_y(k).wait()
    for k in range(1, nd):
        copy_f(k).wait()


def make_filters(inner, cross, lead, held):
    nd, ns = lax.axis_size("node"), lax.axis_size("src")
    sensors, time = held.shape[1:]
    own, mp = lead.shape[2:]
    outer = ns // inner
    vmem = pl.BlockSpec(memory_space=pltpu.VMEM)
    return pl.pallas_call(
        functools.partial(filter_kernel, nd, ns, inner, float(time * nd * ns)),
        out_shape=(
            jax.ShapeDtypeStruct((3, nd, own, sensors), BF16),
            jax.ShapeDtypeStruct((sensors, ns * time), BF16),
        ),
        in_specs=[vmem] * 3,
        out_specs=(vmem, vmem),
        scratch_shapes=[pltpu.VMEM((nd - 1,) + lead.shape[1:], F32)]
        + [pltpu.SemaphoreType.DMA((n,)) for n in (nd - 1, nd - 1, outer, outer, nd - 1, nd - 1)],
        compiler_params=pltpu.CompilerParams(collective_id=1, has_side_effects=True),
        name="filters",
    )(cross, lead, held)


def local(transfer, node_pos, node_layer, layer_cond, tile_center, dip_tile, dip_offset, recording):
    sensors = transfer.shape[0]
    dipoles = dip_tile.shape[0]
    inner = math.gcd(lax.axis_size("src"), 2)
    cross, lead, held = lead_and_cross(
        inner, recording, transfer, node_pos, node_layer[None, :], layer_cond, tile_center, dip_tile[None, :], dip_offset
    )
    filters, samples = make_filters(inner, cross, lead, held)
    out = jnp.dot(filters.reshape(3 * dipoles, sensors), samples, preferred_element_type=F32)
    return out.astype(BF16).reshape(3, dipoles, samples.shape[1])


def solution(mesh):
    return jax.shard_map(
        local,
        mesh=mesh,
        in_specs=(
            P(None, "node"),
            P(None, "node"),
            P("node"),
            P(),
            P(),
            P("src"),
            P(None, "src"),
            P(None, ("node", "src")),
        ),
        out_specs=P(None, "src", "node"),
        check_vma=False,
    )
```

```python
import functools
import math

import jax
import jax.numpy as jnp
from jax import lax
from jax.experimental import pallas as pl
from jax.experimental.pallas import tpu as pltpu
from jax.sharding import PartitionSpec as P

SOFTENING = 0.02
COV_RIDGE = 0.05
GRAM_RIDGE = 0.01
EPSILON = 1e-06
NT = (((1,), (1,)), ((), ()))
F32 = jnp.float32
BF16 = jnp.bfloat16


def round_up(value, unit):
    return -(-value // unit) * unit


def place_dipoles(tile_center, dip_tile, dip_offset):
    tiles, dipoles = tile_center.shape[1], dip_tile.shape[1]
    onehot = (lax.broadcasted_iota(jnp.int32, (tiles, dipoles), 0) == dip_tile).astype(F32)
    rows = jnp.dot(tile_center, onehot, precision=lax.Precision.HIGHEST, preferred_element_type=F32) + dip_offset
    return jnp.concatenate([rows, jnp.zeros((128 - rows.shape[0], dipoles), F32)], axis=0).T


def layer_scale(node_layer, layer_cond):
    scale = jnp.zeros(node_layer.shape, F32)
    for level in range(layer_cond.shape[0]):
        scale = jnp.where(node_layer == level, layer_cond[level], scale)
    return scale


def remote(held, dst, send_sem, recv_sem, **where):
    return pltpu.make_async_remote_copy(
        src_ref=held, dst_ref=dst, send_sem=send_sem, recv_sem=recv_sem,
        device_id=where, device_id_type=pl.DeviceIdType.MESH,
    )


def potential_rows(node, scale, dip, rows):
    dipoles = dip.shape[0]
    parts = [[], [], []]
    for first in range(0, dipoles, rows):
        offsets = [node[c : c + 1, :] - dip[first : first + rows, c : c + 1] for c in range(3)]
        q = offsets[0] * offsets[0] + offsets[1] * offsets[1] + offsets[2] * offsets[2] + SOFTENING
        root = lax.rsqrt(q)
        weights = (scale * root) * (root * root)
        for c in range(3):
            parts[c].append((offsets[c] * weights).astype(BF16))
    return jnp.concatenate(parts[0] + parts[1] + parts[2], axis=0)


def pack_halves(aug, half):
    width = aug.shape[0]
    second = aug[half : 2 * half]
    turned = jnp.concatenate([second, aug[:half], aug[2 * half :]], axis=0)
    top = lax.dot_general(aug[:half], aug, NT, preferred_element_type=F32)
    low = lax.dot_general(second, turned, NT, preferred_element_type=F32)
    rows = lax.broadcasted_iota(jnp.int32, (half, width), 0)
    cols = lax.broadcasted_iota(jnp.int32, (half, width), 1)
    diagonal = jnp.sum(jnp.where(rows == cols, low, 0.0), axis=1, keepdims=True)
    packed = jnp.where(cols >= rows, top, low)
    return jnp.where(cols == 2 * half, diagonal, packed)


def unpack_halves(packed):
    half, width = packed.shape
    flipped = jnp.concatenate([packed, jnp.zeros((width - half, width), F32)], axis=0).T
    rows = lax.broadcasted_iota(jnp.int32, (half, width), 0)
    cols = lax.broadcasted_iota(jnp.int32, (half, width), 1)
    top = jnp.where(cols >= rows, packed, flipped[:half])
    top = jnp.where(cols < 2 * half, top, 0.0)
    corner = jnp.where(rows > cols, packed, flipped[:half])
    corner = jnp.where(rows == cols, packed[:, 2 * half : 2 * half + 1], corner)
    corner = jnp.where(cols < half, corner, 0.0)
    low = jnp.where(cols < half, flipped[half : 2 * half], pltpu.roll(corner, half, 1))
    return jnp.concatenate([top, low, jnp.zeros((width - 2 * half, width), F32)], axis=0)


def lead_kernel(
    nd, ns, inner, half, r, stages,
    rec, transfer, node, layer, cond, centre, tile, offset, cross_out, lead_out, z_out,
    dip, aug, acc, buf, got_a, part, got_b, fin, res,
    s_a, r_a, s_b, r_b, s_c, r_c, s_d, r_d, s_z, r_z,
):
    step = pl.program_id(0)
    me_n, me_s = lax.axis_index("node"), lax.axis_index("src")
    sensors = rec.shape[0]
    dipoles = dip.shape[0]
    mp = aug.shape[0]
    outer = ns // inner
    hi, lo = me_s // inner, lax.rem(me_s, inner)
    peer_n = [None] + [lax.rem(me_n + k, nd) for k in range(1, nd)]
    peer_s = [None] + [lax.rem(me_s + k, ns) for k in range(1, ns)]

    def copy_a(k):
        return remote(buf.at[peer_n[k]], got_a.at[k - 1], s_a.at[k - 1], r_a.at[k - 1], node=peer_n[k])

    def copy_b(k):
        return remote(part.at[peer_s[k]], got_b.at[k - 1], s_b.at[k - 1], r_b.at[k - 1], src=peer_s[k])

    def copy_c(k):
        return remote(fin, res.at[me_n, me_s], s_c.at[k - 1], r_c.at[k - 1], src=peer_s[k])

    def copy_d(k):
        return remote(res.at[me_n], res.at[me_n], s_d.at[k - 1], r_d.at[k - 1], node=peer_n[k])

    copy_z = remote(rec, z_out, s_z, r_z, src=lax.rem(hi + 1, outer) * inner + lo)

    @pl.when(step == stages[0])
    def _():
        barrier = pltpu.get_barrier_semaphore()
        for k in range(1, nd):
            pl.semaphore_signal(barrier, inc=1, device_id={"node": peer_n[k]}, device_id_type=pl.DeviceIdType.MESH)
        for k in range(1, ns):
            pl.semaphore_signal(barrier, inc=1, device_id={"src": peer_s[k]}, device_id_type=pl.DeviceIdType.MESH)
        acc[...] = jnp.zeros_like(acc)
        low = sensors // 16 * 16
        tail = lax.broadcasted_iota(jnp.int32, (mp - low, aug.shape[1]), 0) + low
        aug[low:, :] = jnp.where(tail == sensors, 1.0, 0.0).astype(BF16)
        aug[:sensors, :] = rec[...]
        packed = pack_halves(aug[...], half)
        rows = nd * ns * r
        if rows > half:
            packed = jnp.concatenate([packed, jnp.zeros((rows - half, mp), F32)], axis=0)
        for n in range(nd):
            for s in range(ns):
                first = (n * ns + s) * r
                buf[n, s] = packed[first : first + r, :]
        pl.semaphore_wait(barrier, nd - 1 + ns - 1)
        for k in range(1, nd):
            copy_a(k).start()
        copy_z.start()
        dip[...] = place_dipoles(centre[...], tile[...], offset[...])

    @pl.when(step == stages[1])
    def _():
        total = buf[me_n]
        for k in range(1, nd):
            copy_a(k).wait()
            total = total + got_a[k - 1]
        part[...] = total
        for k in range(1, ns):
            copy_b(k).start()

    @pl.when(step == stages[2])
    def _():
        total = part[me_s]
        for k in range(1, ns):
            copy_b(k).wait()
            total = total + got_b[k - 1]
        fin[...] = total
        res[me_n, me_s] = total
        for k in range(1, ns):
            copy_c(k).start()

    @pl.when(step == stages[3])
    def _():
        for k in range(1, ns):
            copy_c(k).wait()
        for k in range(1, nd):
            copy_d(k).start()

    block = transfer.shape[1]
    sub = math.gcd(block, 512)
    dip_now = dip[...]
    scale = layer_scale(layer[...], cond)
    total = None
    for first in range(0, block, sub):
        potential = potential_rows(
            node[:, first : first + sub], scale[:, first : first + sub], dip_now, 32
        )
        product = lax.dot_general(
            transfer[:, first : first + sub], potential, NT, preferred_element_type=F32
        )
        total = product if total is None else total + product
    acc[:sensors, :] += total

    @pl.when(step == stages[4])
    def _():
        flipped = acc[...].T
        own = dipoles // nd
        for n in range(nd):
            for c in range(3):
                first = c * dipoles + n * own
                lead_out[n, c] = flipped[first : first + own, :]
        for k in range(1, nd):
            copy_d(k).wait()
        for n in range(nd):
            for s in range(ns):
                first = (n * ns + s) * r
                cross_out[first : first + r, :] = res[n, s]
        copy_z.wait()


def lead_and_cross(inner, rec, transfer, node, layer, cond, centre, tile, offset):
    nd, ns = lax.axis_size("node"), lax.axis_size("src")
    sensors, time = rec.shape
    nodes = transfer.shape[1]
    dipoles = tile.shape[1]
    outer = ns // inner
    half = round_up(-(-(sensors + 1) // 2), 16)
    mp = round_up(2 * half + 1, 128)
    r = -(-half // (nd * ns))
    block = math.gcd(nodes, 1024)
    steps = nodes // block
    last = steps - 1
    stages = (0, last * 4 // 14, last * 8 // 14, last * 11 // 14, last)
    chunk = (nd, ns, r, mp)
    vmem = pl.BlockSpec(memory_space=pltpu.VMEM)
    return pl.pallas_call(
        functools.partial(lead_kernel, nd, ns, inner, half, r, stages),
        grid=(steps,),
        out_shape=(
            jax.ShapeDtypeStruct((nd * ns * r, mp), F32),
            jax.ShapeDtypeStruct((nd, 3, dipoles // nd, mp), F32),
            jax.ShapeDtypeStruct((sensors, time), BF16),
        ),
        in_specs=[
            vmem,
            pl.BlockSpec((sensors, block), lambda i: (0, i)),
            pl.BlockSpec((3, block), lambda i: (0, i)),
            pl.BlockSpec((1, block), lambda i: (0, i)),
            pl.BlockSpec(memory_space=pltpu.SMEM),
            vmem,
            vmem,
            vmem,
        ],
        out_specs=(vmem, vmem, pl.BlockSpec(memory_space=pl.ANY)),
        scratch_shapes=[
            pltpu.VMEM((dipoles, 128), F32),
            pltpu.VMEM((mp, time), BF16),
            pltpu.VMEM((mp, 3 * dipoles), F32),
            pltpu.VMEM(chunk, F32),
            pltpu.VMEM((nd - 1,) + chunk[1:], F32),
            pltpu.VMEM(chunk[1:], F32),
            pltpu.VMEM((ns - 1,) + chunk[2:], F32),
            pltpu.VMEM(chunk[2:], F32),
            pltpu.VMEM(chunk, F32),
        ]
        + [pltpu.SemaphoreType.DMA((n,)) for n in (nd - 1, nd - 1, ns - 1, ns - 1, ns - 1, ns - 1, nd - 1, nd - 1)]
        + [pltpu.SemaphoreType.DMA] * 2,
        compiler_params=pltpu.CompilerParams(collective_id=0, has_side_effects=True),
        name="lead_cross",
    )(rec, transfer, node, layer, cond, centre, tile, offset)


def dot_full(a, b):
    return jnp.dot(a, b, precision=lax.Precision.HIGHEST, preferred_element_type=F32)


def halves(a):
    high = a.astype(BF16)
    return high, (a - high.astype(F32)).astype(BF16)


def dot_three(a, b):
    (ah, al), (bh, bl) = a, b
    dot = functools.partial(jnp.dot, preferred_element_type=F32)
    return dot(ah, bh) + (dot(ah, bl) + dot(al, bh))


def covariance_inverse(cross, sensors, count, full_steps, midway):
    mp = cross.shape[0]
    rows = lax.broadcasted_iota(jnp.int32, (mp, mp), 0)
    cols = lax.broadcasted_iota(jnp.int32, (mp, mp), 1)
    average = cross[:, sensors : sensors + 1] / count
    sums = cross[sensors : sensors + 1, :]
    cov = (cross - average * sums) / (count - 1.0)
    cov = jnp.where((rows < sensors) & (cols < sensors), cov, 0.0)
    diagonal = rows == cols
    trace = jnp.sum(jnp.sum(jnp.where(diagonal, cov, 0.0), axis=1, keepdims=True), axis=0, keepdims=True)
    ridge = COV_RIDGE / sensors * trace
    centre = 0.5 * trace + ridge
    scaled = cov / centre + jnp.where(diagonal, jnp.where(rows < sensors, ridge / centre, 1.0), 0.0)
    ratio = sensors / COV_RIDGE + 1.0
    h = (ratio - 1.0) / (ratio + 1.0)
    plan = []
    while h > 1e-5:
        plan.append(1.0 / (2.0 - h * h))
        h = h * h / (2.0 - h * h)
    eye = jnp.where(diagonal, 1.0, 0.0)
    x = (4.0 * plan[0]) * eye - (2.0 * plan[0]) * scaled
    scaled_halves = halves(scaled)
    for at, gain in enumerate(plan[1:], 1):
        if at == len(plan) - full_steps:
            midway()
        if at >= len(plan) - full_steps:
            y = dot_full(scaled, x)
            x = dot_full(x, (4.0 * gain) * eye - (2.0 * gain) * y)
        else:
            xh = halves(x)
            y = dot_three(scaled_halves, xh)
            x = dot_three(xh, halves((4.0 * gain) * eye - (2.0 * gain) * y))
    return x / centre


def filter_kernel(
    nd, ns, inner, count,
    cross, lead, rec, near, filt, rec_all,
    got, s_l, r_l, s_y, r_y, s_z, r_z, s_f, r_f,
):
    me_n, me_s = lax.axis_index("node"), lax.axis_index("src")
    outer = ns // inner
    sensors, time = rec.shape
    own = lead.shape[2]
    mp = cross.shape[1]
    hi, lo = me_s // inner, lax.rem(me_s, inner)
    peer_n = [None] + [lax.rem(me_n + k, nd) for k in range(1, nd)]
    peer_z = [None] + [lax.rem(hi + k, outer) * inner + lo for k in range(1, outer)]
    from_z = [me_s] + [lax.rem(hi + outer - k, outer) * inner + lo for k in range(1, outer)]
    peer_y = hi * inner + lax.rem(lo + 1, inner)

    def columns(s):
        return rec_all.at[:, pl.ds(pl.multiple_of(s * time, time), time)]

    def copy_l(k):
        return remote(lead.at[peer_n[k]], got.at[k - 1], s_l.at[k - 1], r_l.at[k - 1], node=peer_n[k])

    def copy_y(k):
        source = rec if k == 0 else near if k == 1 else columns(from_z[k])
        return remote(source, columns(from_z[k]), s_y.at[k], r_y.at[k], src=peer_y)

    def copy_z(k):
        return remote(rec, columns(me_s), s_z.at[k - 2], r_z.at[k - 2], src=peer_z[k])

    def relay(ks):
        for k in ks:
            copy_z(k).wait()
            copy_y(k).start()

    def copy_f(k):
        return remote(filt.at[:, me_n], filt.at[:, me_n], s_f.at[k - 1], r_f.at[k - 1], node=peer_n[k])

    barrier = pltpu.get_barrier_semaphore()
    for k in range(1, nd):
        pl.semaphore_signal(barrier, inc=1, device_id={"node": peer_n[k]}, device_id_type=pl.DeviceIdType.MESH)
    for k in range(1, outer):
        pl.semaphore_signal(barrier, inc=1, device_id={"src": peer_z[k]}, device_id_type=pl.DeviceIdType.MESH)
    pl.semaphore_signal(barrier, inc=1, device_id={"src": peer_y}, device_id_type=pl.DeviceIdType.MESH)
    pl.semaphore_wait(barrier, nd - 1 + outer)

    for k in range(1, nd):
        copy_l(k).start()
    for k in range(2):
        copy_y(k).start()
    later = list(range(outer - 1, 1, -1))
    for k in later:
        copy_z(k).start()
    for k, block in enumerate((rec, near)):
        rec_all[:, pl.ds(pl.multiple_of(from_z[k] * time, time), time)] = block[...]

    half = round_up(-(-(sensors + 1) // 2), 16)
    split = len(later) // 2
    inverse = covariance_inverse(
        unpack_halves(cross[:half, :]), sensors, count, 2, functools.partial(relay, later[:split])
    )
    relay(later[split:])

    field = lead[me_n]
    for k in range(1, nd):
        copy_l(k).wait()
        field = field + got[k - 1]
    square = jnp.sum(jnp.sum(field * field, axis=0), axis=1, keepdims=True) / (3.0 * sensors)
    normed = field / jnp.sqrt(square + EPSILON)[None]
    solved = dot_full(normed.reshape(3 * own, mp), inverse).reshape(3, own, mp)
    gram = {}
    for c in range(3):
        for d in range(c, 3):
            gram[c, d] = jnp.sum(normed[c] * solved[d], axis=1, keepdims=True)
            gram[d, c] = gram[c, d]
    ridge = GRAM_RIDGE * (gram[0, 0] + gram[1, 1] + gram[2, 2]) / 3.0
    for c in range(3):
        gram[c, c] = gram[c, c] + ridge

    def cofactor(row, col):
        a, b, c, d = (row + 1) % 3, (row + 2) % 3, (col + 1) % 3, (col + 2) % 3
        return gram[a, c] * gram[b, d] - gram[a, d] * gram[b, c]

    determinant = gram[0, 0] * cofactor(0, 0) + gram[0, 1] * cofactor(0, 1) + gram[0, 2] * cofactor(0, 2)
    for c in range(3):
        mixed = sum((cofactor(d, c) / determinant) * solved[d] for d in range(3))
        filt[c, me_n] = mixed[:, :sensors].astype(BF16)
    for k in range(1, nd):
        copy_f(k).start()
    for k in range(outer):
        copy_y(k).wait()
    for k in range(1, nd):
        copy_f(k).wait()


def make_filters(inner, cross, lead, rec, near):
    nd, ns = lax.axis_size("node"), lax.axis_size("src")
    sensors, time = rec.shape
    own, mp = lead.shape[2:]
    outer = ns // inner
    vmem = pl.BlockSpec(memory_space=pltpu.VMEM)
    return pl.pallas_call(
        functools.partial(filter_kernel, nd, ns, inner, float(time * nd * ns)),
        out_shape=(
            jax.ShapeDtypeStruct((3, nd, own, sensors), BF16),
            jax.ShapeDtypeStruct((sensors, ns * time), BF16),
        ),
        in_specs=[vmem] * 4,
        out_specs=(vmem, vmem),
        scratch_shapes=[pltpu.VMEM((nd - 1,) + lead.shape[1:], F32)]
        + [pltpu.SemaphoreType.DMA((n,)) for n in (nd - 1, nd - 1, outer, outer, outer - 2, outer - 2, nd - 1, nd - 1)],
        compiler_params=pltpu.CompilerParams(collective_id=1, has_side_effects=True),
        name="filters",
    )(cross, lead, rec, near)


def local(transfer, node_pos, node_layer, layer_cond, tile_center, dip_tile, dip_offset, recording):
    sensors = transfer.shape[0]
    dipoles = dip_tile.shape[0]
    inner = math.gcd(lax.axis_size("src"), 2)
    cross, lead, near = lead_and_cross(
        inner, recording, transfer, node_pos, node_layer[None, :], layer_cond, tile_center, dip_tile[None, :], dip_offset
    )
    filters, samples = make_filters(inner, cross, lead, recording, near)
    out = jnp.dot(filters.reshape(3 * dipoles, sensors), samples, preferred_element_type=F32)
    return out.astype(BF16).reshape(3, dipoles, samples.shape[1])


def solution(mesh):
    return jax.shard_map(
        local,
        mesh=mesh,
        in_specs=(
            P(None, "node"),
            P(None, "node"),
            P("node"),
            P(),
            P(),
            P("src"),
            P(None, "src"),
            P(None, ("node", "src")),
        ),
        out_specs=P(None, "src", "node"),
        check_vma=False,
    )
```

```python
import functools
import math

import jax
import jax.numpy as jnp
from jax import lax
from jax.experimental import pallas as pl
from jax.experimental.pallas import tpu as pltpu
from jax.sharding import PartitionSpec as P

SOFTENING = 0.02
COV_RIDGE = 0.05
GRAM_RIDGE = 0.01
EPSILON = 1e-06
NT = (((1,), (1,)), ((), ()))
F32 = jnp.float32
BF16 = jnp.bfloat16


def round_up(value, unit):
    return -(-value // unit) * unit


def place_dipoles(tile_center, dip_tile, dip_offset):
    tiles, dipoles = tile_center.shape[1], dip_tile.shape[1]
    onehot = (lax.broadcasted_iota(jnp.int32, (tiles, dipoles), 0) == dip_tile).astype(F32)
    rows = jnp.dot(tile_center, onehot, precision=lax.Precision.HIGHEST, preferred_element_type=F32) + dip_offset
    return jnp.concatenate([rows, jnp.zeros((128 - rows.shape[0], dipoles), F32)], axis=0).T


def layer_scale(node_layer, layer_cond):
    scale = jnp.zeros(node_layer.shape, F32)
    for level in range(layer_cond.shape[0]):
        scale = jnp.where(node_layer == level, layer_cond[level], scale)
    return scale


def remote(held, dst, send_sem, recv_sem, **where):
    return pltpu.make_async_remote_copy(
        src_ref=held, dst_ref=dst, send_sem=send_sem, recv_sem=recv_sem,
        device_id=where, device_id_type=pl.DeviceIdType.MESH,
    )


def potential_rows(node, scale, dip, rows):
    dipoles = dip.shape[0]
    parts = [[], [], []]
    for first in range(0, dipoles, rows):
        offsets = [node[c : c + 1, :] - dip[first : first + rows, c : c + 1] for c in range(3)]
        q = offsets[0] * offsets[0] + offsets[1] * offsets[1] + offsets[2] * offsets[2] + SOFTENING
        root = lax.rsqrt(q)
        weights = (scale * root) * (root * root)
        for c in range(3):
            parts[c].append((offsets[c] * weights).astype(BF16))
    return jnp.concatenate(parts[0] + parts[1] + parts[2], axis=0)


def pack_halves(aug, half):
    width = aug.shape[0]
    second = aug[half : 2 * half]
    turned = jnp.concatenate([second, aug[:half], aug[2 * half :]], axis=0)
    top = lax.dot_general(aug[:half], aug, NT, preferred_element_type=F32)
    low = lax.dot_general(second, turned, NT, preferred_element_type=F32)
    rows = lax.broadcasted_iota(jnp.int32, (half, width), 0)
    cols = lax.broadcasted_iota(jnp.int32, (half, width), 1)
    diagonal = jnp.sum(jnp.where(rows == cols, low, 0.0), axis=1, keepdims=True)
    packed = jnp.where(cols >= rows, top, low)
    return jnp.where(cols == 2 * half, diagonal, packed)


def unpack_halves(packed):
    half, width = packed.shape
    flipped = jnp.concatenate([packed, jnp.zeros((width - half, width), F32)], axis=0).T
    rows = lax.broadcasted_iota(jnp.int32, (half, width), 0)
    cols = lax.broadcasted_iota(jnp.int32, (half, width), 1)
    top = jnp.where(cols >= rows, packed, flipped[:half])
    top = jnp.where(cols < 2 * half, top, 0.0)
    corner = jnp.where(rows > cols, packed, flipped[:half])
    corner = jnp.where(rows == cols, packed[:, 2 * half : 2 * half + 1], corner)
    corner = jnp.where(cols < half, corner, 0.0)
    low = jnp.where(cols < half, flipped[half : 2 * half], pltpu.roll(corner, half, 1))
    return jnp.concatenate([top, low, jnp.zeros((width - 2 * half, width), F32)], axis=0)


def near_hops(outer):
    return sorted({1, outer - 1})


def lead_kernel(
    nd, ns, inner, half, r, stages,
    rec, transfer, node, layer, cond, centre, tile, offset, cross_out, lead_out, z_out,
    dip, aug, acc, pair, got_p, buf, got_a, part, got_b, fin, res,
    s_a, r_a, s_b, r_b, s_c, r_c, s_d, r_d, s_z, r_z, s_p, r_p,
):
    step = pl.program_id(0)
    me_n, me_s = lax.axis_index("node"), lax.axis_index("src")
    sensors = rec.shape[0]
    dipoles = dip.shape[0]
    mp = aug.shape[0]
    outer = ns // inner
    hi, lo = me_s // inner, lax.rem(me_s, inner)
    peer_n = [None] + [lax.rem(me_n + k, nd) for k in range(1, nd)]
    peer_s = [None] + [lax.rem(me_s + k, ns) for k in range(1, ns)]

    def copy_a(k):
        return remote(buf.at[peer_n[k]], got_a.at[k - 1], s_a.at[k - 1], r_a.at[k - 1], node=peer_n[k])

    def copy_b(k):
        return remote(part.at[peer_s[k]], got_b.at[k - 1], s_b.at[k - 1], r_b.at[k - 1], src=peer_s[k])

    def copy_c(k):
        return remote(fin, res.at[me_n, me_s], s_c.at[k - 1], r_c.at[k - 1], src=peer_s[k])

    def copy_d(k):
        return remote(res.at[me_n], res.at[me_n], s_d.at[k - 1], r_d.at[k - 1], node=peer_n[k])

    near = near_hops(outer)

    def copy_z(at):
        peer = lax.rem(hi + near[at], outer) * inner + lo
        return remote(rec, z_out.at[at], s_z.at[at], r_z.at[at], src=peer)

    core = lax.rem(me_n, 2)
    copy_p = remote(pair.at[1 - core], got_p, s_p, r_p, node=me_n + 1 - 2 * core)

    @pl.when(step == stages[0])
    def _():
        barrier = pltpu.get_barrier_semaphore()
        for k in range(1, nd):
            pl.semaphore_signal(barrier, inc=1, device_id={"node": peer_n[k]}, device_id_type=pl.DeviceIdType.MESH)
        for k in range(1, ns):
            pl.semaphore_signal(barrier, inc=1, device_id={"src": peer_s[k]}, device_id_type=pl.DeviceIdType.MESH)
        acc[...] = jnp.zeros_like(acc)
        low = sensors // 16 * 16
        tail = lax.broadcasted_iota(jnp.int32, (mp - low, aug.shape[1]), 0) + low
        aug[low:, :] = jnp.where(tail == sensors, 1.0, 0.0).astype(BF16)
        aug[:sensors, :] = rec[...]
        packed = pack_halves(aug[...], half)
        rows = nd * ns * r
        if rows > half:
            packed = jnp.concatenate([packed, jnp.zeros((rows - half, mp), F32)], axis=0)
        for n in range(nd):
            for s in range(ns):
                first = (n * ns + s) * r
                buf[n, s] = packed[first : first + r, :]
        pl.semaphore_wait(barrier, nd - 1 + ns - 1)
        for k in range(1, nd):
            copy_a(k).start()
        copy_z(0).start()
        dip[...] = place_dipoles(centre[...], tile[...], offset[...])

    @pl.when(step == stages[1])
    def _():
        total = buf[me_n]
        for k in range(1, nd):
            copy_a(k).wait()
            total = total + got_a[k - 1]
        part[...] = total
        for k in range(1, ns):
            copy_b(k).start()

    @pl.when(step == stages[2])
    def _():
        total = part[me_s]
        for k in range(1, ns):
            copy_b(k).wait()
            total = total + got_b[k - 1]
        fin[...] = total
        res[me_n, me_s] = total
        for k in range(1, ns):
            copy_c(k).start()

    @pl.when(step == stages[3])
    def _():
        for k in range(1, ns):
            copy_c(k).wait()
        for k in range(1, nd):
            copy_d(k).start()
        for at in range(1, len(near)):
            copy_z(at).start()

    block = transfer.shape[1]
    sub = math.gcd(block, 512)
    dip_now = dip[...]
    scale = layer_scale(layer[...], cond)
    total = None
    for first in range(0, block, sub):
        potential = potential_rows(
            node[:, first : first + sub], scale[:, first : first + sub], dip_now, 32
        )
        product = lax.dot_general(
            transfer[:, first : first + sub], potential, NT, preferred_element_type=F32
        )
        total = product if total is None else total + product
    acc[:sensors, :] += total

    @pl.when(step == stages[4])
    def _():
        flipped = acc[...].T
        own = dipoles // 2
        for n in range(2):
            for c in range(3):
                first = c * dipoles + n * own
                pair[n, c] = flipped[first : first + own, :]
        copy_p.start()
        for k in range(1, nd):
            copy_d(k).wait()
        for n in range(nd):
            for s in range(ns):
                first = (n * ns + s) * r
                cross_out[first : first + r, :] = res[n, s]
        copy_p.wait()
        lead_out[...] = pair[core] + got_p[...]
        for at in range(len(near)):
            copy_z(at).wait()


def lead_and_cross(inner, rec, transfer, node, layer, cond, centre, tile, offset):
    nd, ns = lax.axis_size("node"), lax.axis_size("src")
    sensors, time = rec.shape
    nodes = transfer.shape[1]
    dipoles = tile.shape[1]
    outer = ns // inner
    half = round_up(-(-(sensors + 1) // 2), 16)
    mp = round_up(2 * half + 1, 128)
    r = -(-half // (nd * ns))
    block = math.gcd(nodes, 1024)
    steps = nodes // block
    last = steps - 1
    stages = (0, last * 4 // 14, last * 8 // 14, last * 11 // 14, last)
    chunk = (nd, ns, r, mp)
    vmem = pl.BlockSpec(memory_space=pltpu.VMEM)
    return pl.pallas_call(
        functools.partial(lead_kernel, nd, ns, inner, half, r, stages),
        grid=(steps,),
        out_shape=(
            jax.ShapeDtypeStruct((nd * ns * r, mp), F32),
            jax.ShapeDtypeStruct((3, dipoles // 2, mp), F32),
            jax.ShapeDtypeStruct((len(near_hops(outer)), sensors, time), BF16),
        ),
        in_specs=[
            vmem,
            pl.BlockSpec((sensors, block), lambda i: (0, i)),
            pl.BlockSpec((3, block), lambda i: (0, i)),
            pl.BlockSpec((1, block), lambda i: (0, i)),
            pl.BlockSpec(memory_space=pltpu.SMEM),
            vmem,
            vmem,
            vmem,
        ],
        out_specs=(vmem, vmem, pl.BlockSpec(memory_space=pl.ANY)),
        scratch_shapes=[
            pltpu.VMEM((dipoles, 128), F32),
            pltpu.VMEM((mp, time), BF16),
            pltpu.VMEM((mp, 3 * dipoles), F32),
            pltpu.VMEM((2, 3, dipoles // 2, mp), F32),
            pltpu.VMEM((3, dipoles // 2, mp), F32),
            pltpu.VMEM(chunk, F32),
            pltpu.VMEM((nd - 1,) + chunk[1:], F32),
            pltpu.VMEM(chunk[1:], F32),
            pltpu.VMEM((ns - 1,) + chunk[2:], F32),
            pltpu.VMEM(chunk[2:], F32),
            pltpu.VMEM(chunk, F32),
        ]
        + [pltpu.SemaphoreType.DMA((n,)) for n in (nd - 1, nd - 1, ns - 1, ns - 1, ns - 1, ns - 1, nd - 1, nd - 1)]
        + [pltpu.SemaphoreType.DMA((len(near_hops(outer)),))] * 2
        + [pltpu.SemaphoreType.DMA] * 2,
        compiler_params=pltpu.CompilerParams(collective_id=0, has_side_effects=True),
        name="lead_cross",
    )(rec, transfer, node, layer, cond, centre, tile, offset)


def dot_full(a, b):
    return jnp.dot(a, b, precision=lax.Precision.HIGHEST, preferred_element_type=F32)


def halves(a):
    high = a.astype(BF16)
    return high, (a - high.astype(F32)).astype(BF16)


def dot_three(a, b):
    (ah, al), (bh, bl) = a, b
    dot = functools.partial(jnp.dot, preferred_element_type=F32)
    return dot(ah, bh) + (dot(ah, bl) + dot(al, bh))


def covariance_inverse(cross, sensors, count, full_steps, midway):
    mp = cross.shape[0]
    rows = lax.broadcasted_iota(jnp.int32, (mp, mp), 0)
    cols = lax.broadcasted_iota(jnp.int32, (mp, mp), 1)
    average = cross[:, sensors : sensors + 1] / count
    sums = cross[sensors : sensors + 1, :]
    cov = (cross - average * sums) / (count - 1.0)
    cov = jnp.where((rows < sensors) & (cols < sensors), cov, 0.0)
    diagonal = rows == cols
    trace = jnp.sum(jnp.sum(jnp.where(diagonal, cov, 0.0), axis=1, keepdims=True), axis=0, keepdims=True)
    ridge = COV_RIDGE / sensors * trace
    centre = 0.5 * trace + ridge
    scaled = cov / centre + jnp.where(diagonal, jnp.where(rows < sensors, ridge / centre, 1.0), 0.0)
    ratio = sensors / COV_RIDGE + 1.0
    h = (ratio - 1.0) / (ratio + 1.0)
    plan = []
    while h > 1e-5:
        plan.append(1.0 / (2.0 - h * h))
        h = h * h / (2.0 - h * h)
    eye = jnp.where(diagonal, 1.0, 0.0)
    x = (4.0 * plan[0]) * eye - (2.0 * plan[0]) * scaled
    scaled_halves = halves(scaled)
    for at, gain in enumerate(plan[1:], 1):
        if at == len(plan) - full_steps:
            midway()
        if at >= len(plan) - full_steps:
            y = dot_full(scaled, x)
            x = dot_full(x, (4.0 * gain) * eye - (2.0 * gain) * y)
        else:
            xh = halves(x)
            y = dot_three(scaled_halves, xh)
            x = dot_three(xh, halves((4.0 * gain) * eye - (2.0 * gain) * y))
    return x / centre


def filter_kernel(
    nd, ns, inner, count,
    cross, lead, rec, near, filt, rec_all,
    got, s_l, r_l, s_y, r_y, s_z, r_z, s_f, r_f,
):
    me_n, me_s = lax.axis_index("node"), lax.axis_index("src")
    outer = ns // inner
    sensors, time = rec.shape
    own = lead.shape[1]
    mp = cross.shape[1]
    hi, lo = me_s // inner, lax.rem(me_s, inner)
    core, chips = lax.rem(me_n, 2), nd // 2
    peer_x = [None] + [lax.rem(me_n // 2 + k, chips) * 2 + core for k in range(1, chips)]
    partner = me_n + 1 - 2 * core
    hops = near_hops(outer)
    peer_z = [None] + [lax.rem(hi + k, outer) * inner + lo for k in range(1, outer)]
    from_z = [me_s] + [lax.rem(hi + outer - k, outer) * inner + lo for k in range(1, outer)]
    peer_y = hi * inner + lax.rem(lo + 1, inner)

    def columns(s):
        return rec_all.at[:, pl.ds(pl.multiple_of(s * time, time), time)]

    def copy_l(k):
        return remote(lead, got.at[k - 1], s_l.at[k - 1], r_l.at[k - 1], node=peer_x[k])

    def copy_y(k):
        source = rec if k == 0 else near.at[hops.index(k)] if k in hops else columns(from_z[k])
        return remote(source, columns(from_z[k]), s_y.at[k], r_y.at[k], src=peer_y)

    def copy_z(k):
        return remote(rec, columns(me_s), s_z.at[k - 1], r_z.at[k - 1], src=peer_z[k])

    def relay(ks):
        for k in ks:
            copy_z(k).wait()
            copy_y(k).start()

    copy_f = remote(filt.at[:, core], filt.at[:, core], s_f, r_f, node=partner)

    barrier = pltpu.get_barrier_semaphore()
    for peer in peer_x[1:] + [partner]:
        pl.semaphore_signal(barrier, inc=1, device_id={"node": peer}, device_id_type=pl.DeviceIdType.MESH)
    for k in range(1, outer):
        pl.semaphore_signal(barrier, inc=1, device_id={"src": peer_z[k]}, device_id_type=pl.DeviceIdType.MESH)
    pl.semaphore_signal(barrier, inc=1, device_id={"src": peer_y}, device_id_type=pl.DeviceIdType.MESH)
    pl.semaphore_wait(barrier, chips + outer)

    for k in range(1, chips):
        copy_l(k).start()
    for k in [0] + hops:
        copy_y(k).start()
    later = [k for k in range(1, outer) if k not in hops]
    for k in later:
        copy_z(k).start()
    for k in [0] + hops:
        first = pl.multiple_of(from_z[k] * time, time)
        rec_all[:, pl.ds(first, time)] = rec[...] if k == 0 else near[hops.index(k)]

    half = round_up(-(-(sensors + 1) // 2), 16)
    inverse = covariance_inverse(
        unpack_halves(cross[:half, :]), sensors, count, 2, functools.partial(relay, later)
    )
    field = lead[...]
    for k in range(1, chips):
        copy_l(k).wait()
        field = field + got[k - 1]
    square = jnp.sum(jnp.sum(field * field, axis=0), axis=1, keepdims=True) / (3.0 * sensors)
    normed = field / jnp.sqrt(square + EPSILON)[None]
    solved = dot_full(normed.reshape(3 * own, mp), inverse).reshape(3, own, mp)
    gram = {}
    for c in range(3):
        for d in range(c, 3):
            gram[c, d] = jnp.sum(normed[c] * solved[d], axis=1, keepdims=True)
            gram[d, c] = gram[c, d]
    ridge = GRAM_RIDGE * (gram[0, 0] + gram[1, 1] + gram[2, 2]) / 3.0
    for c in range(3):
        gram[c, c] = gram[c, c] + ridge

    def cofactor(row, col):
        a, b, c, d = (row + 1) % 3, (row + 2) % 3, (col + 1) % 3, (col + 2) % 3
        return gram[a, c] * gram[b, d] - gram[a, d] * gram[b, c]

    determinant = gram[0, 0] * cofactor(0, 0) + gram[0, 1] * cofactor(0, 1) + gram[0, 2] * cofactor(0, 2)
    for c in range(3):
        mixed = sum((cofactor(d, c) / determinant) * solved[d] for d in range(3))
        filt[c, core] = mixed[:, :sensors].astype(BF16)
    copy_f.start()
    for k in range(outer):
        copy_y(k).wait()
    copy_f.wait()


def make_filters(inner, cross, lead, rec, near):
    nd, ns = lax.axis_size("node"), lax.axis_size("src")
    sensors, time = rec.shape
    own, mp = lead.shape[1:]
    outer = ns // inner
    vmem = pl.BlockSpec(memory_space=pltpu.VMEM)
    return pl.pallas_call(
        functools.partial(filter_kernel, nd, ns, inner, float(time * nd * ns)),
        out_shape=(
            jax.ShapeDtypeStruct((3, 2, own, sensors), BF16),
            jax.ShapeDtypeStruct((sensors, ns * time), BF16),
        ),
        in_specs=[vmem] * 4,
        out_specs=(vmem, vmem),
        scratch_shapes=[pltpu.VMEM((max(nd // 2 - 1, 1),) + lead.shape, F32)]
        + [pltpu.SemaphoreType.DMA((n,)) for n in (max(nd // 2 - 1, 1),) * 2 + (outer,) * 4]
        + [pltpu.SemaphoreType.DMA] * 2,
        compiler_params=pltpu.CompilerParams(collective_id=1, has_side_effects=True),
        name="filters",
    )(cross, lead, rec, near)


def local(transfer, node_pos, node_layer, layer_cond, tile_center, dip_tile, dip_offset, recording):
    sensors = transfer.shape[0]
    dipoles = dip_tile.shape[0]
    inner = math.gcd(lax.axis_size("src"), 2)
    cross, lead, near = lead_and_cross(
        inner, recording, transfer, node_pos, node_layer[None, :], layer_cond, tile_center, dip_tile[None, :], dip_offset
    )
    filters, samples = make_filters(inner, cross, lead, recording, near)
    out = jnp.dot(filters.reshape(3 * dipoles, sensors), samples, preferred_element_type=F32)
    return out.astype(BF16).reshape(3, dipoles, samples.shape[1])


def solution(mesh):
    return jax.shard_map(
        local,
        mesh=mesh,
        in_specs=(
            P(None, "node"),
            P(None, "node"),
            P("node"),
            P(),
            P(),
            P("src"),
            P(None, "src"),
            P(None, ("node", "src")),
        ),
        out_specs=P(None, "src", "node"),
        check_vma=False,
    )
```

```python
import functools
import math

import jax
import jax.numpy as jnp
from jax import lax
from jax.experimental import pallas as pl
from jax.experimental.pallas import tpu as pltpu
from jax.sharding import PartitionSpec as P

SOFTENING = 0.02
COV_RIDGE = 0.05
GRAM_RIDGE = 0.01
EPSILON = 1e-06
NT = (((1,), (1,)), ((), ()))
F32 = jnp.float32
BF16 = jnp.bfloat16


def round_up(value, unit):
    return -(-value // unit) * unit


def place_dipoles(tile_center, dip_tile, dip_offset):
    tiles, dipoles = tile_center.shape[1], dip_tile.shape[1]
    onehot = (lax.broadcasted_iota(jnp.int32, (tiles, dipoles), 0) == dip_tile).astype(F32)
    rows = jnp.dot(tile_center, onehot, precision=lax.Precision.HIGHEST, preferred_element_type=F32) + dip_offset
    return jnp.concatenate([rows, jnp.zeros((128 - rows.shape[0], dipoles), F32)], axis=0).T


def layer_scale(node_layer, layer_cond):
    scale = jnp.zeros(node_layer.shape, F32)
    for level in range(layer_cond.shape[0]):
        scale = jnp.where(node_layer == level, layer_cond[level], scale)
    return scale


def remote(held, dst, send_sem, recv_sem, **where):
    return pltpu.make_async_remote_copy(
        src_ref=held, dst_ref=dst, send_sem=send_sem, recv_sem=recv_sem,
        device_id=where, device_id_type=pl.DeviceIdType.MESH,
    )


def potential_rows(node, scale, dip, rows):
    dipoles = dip.shape[0]
    parts = [[], [], []]
    for first in range(0, dipoles, rows):
        offsets = [node[c : c + 1, :] - dip[first : first + rows, c : c + 1] for c in range(3)]
        q = offsets[0] * offsets[0] + offsets[1] * offsets[1] + offsets[2] * offsets[2] + SOFTENING
        root = lax.rsqrt(q)
        weights = (scale * root) * (root * root)
        for c in range(3):
            parts[c].append((offsets[c] * weights).astype(BF16))
    return jnp.concatenate(parts[0] + parts[1] + parts[2], axis=0)


def pack_halves(aug, half):
    width = aug.shape[0]
    second = aug[half : 2 * half]
    turned = jnp.concatenate([second, aug[:half], aug[2 * half :]], axis=0)
    top = lax.dot_general(aug[:half], aug, NT, preferred_element_type=F32)
    low = lax.dot_general(second, turned, NT, preferred_element_type=F32)
    rows = lax.broadcasted_iota(jnp.int32, (half, width), 0)
    cols = lax.broadcasted_iota(jnp.int32, (half, width), 1)
    diagonal = jnp.sum(jnp.where(rows == cols, low, 0.0), axis=1, keepdims=True)
    packed = jnp.where(cols >= rows, top, low)
    return jnp.where(cols == 2 * half, diagonal, packed)


def unpack_halves(packed):
    half, width = packed.shape
    flipped = jnp.concatenate([packed, jnp.zeros((width - half, width), F32)], axis=0).T
    rows = lax.broadcasted_iota(jnp.int32, (half, width), 0)
    cols = lax.broadcasted_iota(jnp.int32, (half, width), 1)
    top = jnp.where(cols >= rows, packed, flipped[:half])
    top = jnp.where(cols < 2 * half, top, 0.0)
    corner = jnp.where(rows > cols, packed, flipped[:half])
    corner = jnp.where(rows == cols, packed[:, 2 * half : 2 * half + 1], corner)
    corner = jnp.where(cols < half, corner, 0.0)
    low = jnp.where(cols < half, flipped[half : 2 * half], pltpu.roll(corner, half, 1))
    return jnp.concatenate([top, low, jnp.zeros((width - 2 * half, width), F32)], axis=0)


def near_hops(outer):
    return sorted({1, outer - 1})


def lead_kernel(
    nd, ns, inner, half, r, stages,
    rec, transfer, node, layer, cond, centre, tile, offset, cross_out, lead_out, z_out,
    dip, aug, acc, pair, got_p, buf, got_a, part, got_b, fin, res,
    s_a, r_a, s_b, r_b, s_c, r_c, s_d, r_d, s_z, r_z, s_p, r_p,
):
    step = pl.program_id(0)
    me_n, me_s = lax.axis_index("node"), lax.axis_index("src")
    sensors = rec.shape[0]
    dipoles = dip.shape[0]
    mp = aug.shape[0]
    outer = ns // inner
    hi, lo = me_s // inner, lax.rem(me_s, inner)
    peer_n = [None] + [lax.rem(me_n + k, nd) for k in range(1, nd)]
    peer_s = [None] + [lax.rem(me_s + k, ns) for k in range(1, ns)]

    def copy_a(k):
        return remote(buf.at[peer_n[k]], got_a.at[k - 1], s_a.at[k - 1], r_a.at[k - 1], node=peer_n[k])

    def copy_b(k):
        return remote(part.at[peer_s[k]], got_b.at[k - 1], s_b.at[k - 1], r_b.at[k - 1], src=peer_s[k])

    def copy_c(k):
        return remote(fin, res.at[me_n, me_s], s_c.at[k - 1], r_c.at[k - 1], src=peer_s[k])

    def copy_d(k):
        return remote(res.at[me_n], res.at[me_n], s_d.at[k - 1], r_d.at[k - 1], node=peer_n[k])

    near = near_hops(outer)

    def copy_z(at):
        peer = lax.rem(hi + near[at], outer) * inner + lo
        return remote(rec, z_out.at[at], s_z.at[at], r_z.at[at], src=peer)

    core = lax.rem(me_n, 2)
    copy_p = remote(pair.at[1 - core], got_p, s_p, r_p, node=me_n + 1 - 2 * core)

    @pl.when(step == stages[0])
    def _():
        barrier = pltpu.get_barrier_semaphore()
        for k in range(1, nd):
            pl.semaphore_signal(barrier, inc=1, device_id={"node": peer_n[k]}, device_id_type=pl.DeviceIdType.MESH)
        for k in range(1, ns):
            pl.semaphore_signal(barrier, inc=1, device_id={"src": peer_s[k]}, device_id_type=pl.DeviceIdType.MESH)
        acc[...] = jnp.zeros_like(acc)
        low = sensors // 16 * 16
        tail = lax.broadcasted_iota(jnp.int32, (mp - low, aug.shape[1]), 0) + low
        aug[low:, :] = jnp.where(tail == sensors, 1.0, 0.0).astype(BF16)
        aug[:sensors, :] = rec[...]
        packed = pack_halves(aug[...], half)
        rows = nd * ns * r
        if rows > half:
            packed = jnp.concatenate([packed, jnp.zeros((rows - half, mp), F32)], axis=0)
        for n in range(nd):
            for s in range(ns):
                first = (n * ns + s) * r
                buf[n, s] = packed[first : first + r, :]
        pl.semaphore_wait(barrier, nd - 1 + ns - 1)
        for k in range(1, nd):
            copy_a(k).start()
        copy_z(0).start()
        dip[...] = place_dipoles(centre[...], tile[...], offset[...])

    @pl.when(step == stages[1])
    def _():
        total = buf[me_n]
        for k in range(1, nd):
            copy_a(k).wait()
            total = total + got_a[k - 1]
        part[...] = total
        for k in range(1, ns):
            copy_b(k).start()

    @pl.when(step == stages[2])
    def _():
        total = part[me_s]
        for k in range(1, ns):
            copy_b(k).wait()
            total = total + got_b[k - 1]
        fin[...] = total
        res[me_n, me_s] = total
        for k in range(1, ns):
            copy_c(k).start()
        for at in range(1, len(near)):
            copy_z(at).start()

    @pl.when(step == stages[3])
    def _():
        for k in range(1, ns):
            copy_c(k).wait()
        for k in range(1, nd):
            copy_d(k).start()

    block = transfer.shape[1]
    sub = math.gcd(block, 512)
    dip_now = dip[...]
    scale = layer_scale(layer[...], cond)
    total = None
    for first in range(0, block, sub):
        potential = potential_rows(
            node[:, first : first + sub], scale[:, first : first + sub], dip_now, 32
        )
        product = lax.dot_general(
            transfer[:, first : first + sub], potential, NT, preferred_element_type=F32
        )
        total = product if total is None else total + product
    acc[:sensors, :] += total

    @pl.when(step == stages[4])
    def _():
        flipped = acc[...].T
        own = dipoles // 2
        for n in range(2):
            for c in range(3):
                first = c * dipoles + n * own
                pair[n, c] = flipped[first : first + own, :]
        copy_p.start()
        for k in range(1, nd):
            copy_d(k).wait()
        for n in range(nd):
            for s in range(ns):
                first = (n * ns + s) * r
                cross_out[first : first + r, :] = res[n, s]
        copy_p.wait()
        lead_out[...] = pair[core] + got_p[...]
        for at in range(len(near)):
            copy_z(at).wait()


def lead_and_cross(inner, rec, transfer, node, layer, cond, centre, tile, offset):
    nd, ns = lax.axis_size("node"), lax.axis_size("src")
    sensors, time = rec.shape
    nodes = transfer.shape[1]
    dipoles = tile.shape[1]
    outer = ns // inner
    half = round_up(-(-(sensors + 1) // 2), 16)
    mp = round_up(2 * half + 1, 128)
    r = -(-half // (nd * ns))
    block = math.gcd(nodes, 1024)
    steps = nodes // block
    last = steps - 1
    stages = (0, last * 4 // 14, last * 8 // 14, last * 11 // 14, last)
    chunk = (nd, ns, r, mp)
    vmem = pl.BlockSpec(memory_space=pltpu.VMEM)
    return pl.pallas_call(
        functools.partial(lead_kernel, nd, ns, inner, half, r, stages),
        grid=(steps,),
        out_shape=(
            jax.ShapeDtypeStruct((nd * ns * r, mp), F32),
            jax.ShapeDtypeStruct((3, dipoles // 2, mp), F32),
            jax.ShapeDtypeStruct((len(near_hops(outer)), sensors, time), BF16),
        ),
        in_specs=[
            vmem,
            pl.BlockSpec((sensors, block), lambda i: (0, i)),
            pl.BlockSpec((3, block), lambda i: (0, i)),
            pl.BlockSpec((1, block), lambda i: (0, i)),
            pl.BlockSpec(memory_space=pltpu.SMEM),
            vmem,
            vmem,
            vmem,
        ],
        out_specs=(vmem, vmem, pl.BlockSpec(memory_space=pl.ANY)),
        scratch_shapes=[
            pltpu.VMEM((dipoles, 128), F32),
            pltpu.VMEM((mp, time), BF16),
            pltpu.VMEM((mp, 3 * dipoles), F32),
            pltpu.VMEM((2, 3, dipoles // 2, mp), F32),
            pltpu.VMEM((3, dipoles // 2, mp), F32),
            pltpu.VMEM(chunk, F32),
            pltpu.VMEM((nd - 1,) + chunk[1:], F32),
            pltpu.VMEM(chunk[1:], F32),
            pltpu.VMEM((ns - 1,) + chunk[2:], F32),
            pltpu.VMEM(chunk[2:], F32),
            pltpu.VMEM(chunk, F32),
        ]
        + [pltpu.SemaphoreType.DMA((n,)) for n in (nd - 1, nd - 1, ns - 1, ns - 1, ns - 1, ns - 1, nd - 1, nd - 1)]
        + [pltpu.SemaphoreType.DMA((len(near_hops(outer)),))] * 2
        + [pltpu.SemaphoreType.DMA] * 2,
        compiler_params=pltpu.CompilerParams(collective_id=0, has_side_effects=True),
        name="lead_cross",
    )(rec, transfer, node, layer, cond, centre, tile, offset)


def dot_full(a, b):
    return jnp.dot(a, b, precision=lax.Precision.HIGHEST, preferred_element_type=F32)


def halves(a):
    high = a.astype(BF16)
    return high, (a - high.astype(F32)).astype(BF16)


def dot_three(a, b):
    (ah, al), (bh, bl) = a, b
    dot = functools.partial(jnp.dot, preferred_element_type=F32)
    return dot(ah, bh) + (dot(ah, bl) + dot(al, bh))


def covariance_inverse(cross, sensors, count, full_steps, midway):
    mp = cross.shape[0]
    rows = lax.broadcasted_iota(jnp.int32, (mp, mp), 0)
    cols = lax.broadcasted_iota(jnp.int32, (mp, mp), 1)
    average = cross[:, sensors : sensors + 1] / count
    sums = cross[sensors : sensors + 1, :]
    cov = (cross - average * sums) / (count - 1.0)
    cov = jnp.where((rows < sensors) & (cols < sensors), cov, 0.0)
    diagonal = rows == cols
    trace = jnp.sum(jnp.sum(jnp.where(diagonal, cov, 0.0), axis=1, keepdims=True), axis=0, keepdims=True)
    ridge = COV_RIDGE / sensors * trace
    centre = 0.5 * trace + ridge
    scaled = cov / centre + jnp.where(diagonal, jnp.where(rows < sensors, ridge / centre, 1.0), 0.0)
    ratio = sensors / COV_RIDGE + 1.0
    h = (ratio - 1.0) / (ratio + 1.0)
    plan = []
    while h > 1e-5:
        plan.append(1.0 / (2.0 - h * h))
        h = h * h / (2.0 - h * h)
    eye = jnp.where(diagonal, 1.0, 0.0)
    x = (4.0 * plan[0]) * eye - (2.0 * plan[0]) * scaled
    scaled_halves = halves(scaled)
    for at, gain in enumerate(plan[1:], 1):
        if at == len(plan) - full_steps:
            midway()
        if at >= len(plan) - full_steps:
            y = dot_full(scaled, x)
            x = dot_full(x, (4.0 * gain) * eye - (2.0 * gain) * y)
        else:
            xh = halves(x)
            y = dot_three(scaled_halves, xh)
            x = dot_three(xh, halves((4.0 * gain) * eye - (2.0 * gain) * y))
    return x / centre


def filter_kernel(
    nd, ns, inner, count,
    cross, lead, rec, near, filt, rec_all,
    got, s_l, r_l, s_y, r_y, s_z, r_z, s_f, r_f,
):
    me_n, me_s = lax.axis_index("node"), lax.axis_index("src")
    outer = ns // inner
    sensors, time = rec.shape
    own = lead.shape[1]
    mp = cross.shape[1]
    hi, lo = me_s // inner, lax.rem(me_s, inner)
    core, chips = lax.rem(me_n, 2), nd // 2
    peer_x = [None] + [lax.rem(me_n // 2 + k, chips) * 2 + core for k in range(1, chips)]
    partner = me_n + 1 - 2 * core
    hops = near_hops(outer)
    peer_z = [None] + [lax.rem(hi + k, outer) * inner + lo for k in range(1, outer)]
    from_z = [me_s] + [lax.rem(hi + outer - k, outer) * inner + lo for k in range(1, outer)]
    peer_y = hi * inner + lax.rem(lo + 1, inner)

    def columns(s):
        return rec_all.at[:, pl.ds(pl.multiple_of(s * time, time), time)]

    def copy_l(k):
        return remote(lead, got.at[k - 1], s_l.at[k - 1], r_l.at[k - 1], node=peer_x[k])

    def copy_y(k):
        source = rec if k == 0 else near.at[hops.index(k)] if k in hops else columns(from_z[k])
        return remote(source, columns(from_z[k]), s_y.at[k], r_y.at[k], src=peer_y)

    def copy_z(k):
        return remote(rec, columns(me_s), s_z.at[k - 1], r_z.at[k - 1], src=peer_z[k])

    def relay(ks):
        for k in ks:
            copy_z(k).wait()
            copy_y(k).start()

    copy_f = remote(filt.at[:, core], filt.at[:, core], s_f, r_f, node=partner)

    barrier = pltpu.get_barrier_semaphore()
    for peer in peer_x[1:] + [partner]:
        pl.semaphore_signal(barrier, inc=1, device_id={"node": peer}, device_id_type=pl.DeviceIdType.MESH)
    for k in range(1, outer):
        pl.semaphore_signal(barrier, inc=1, device_id={"src": peer_z[k]}, device_id_type=pl.DeviceIdType.MESH)
    pl.semaphore_signal(barrier, inc=1, device_id={"src": peer_y}, device_id_type=pl.DeviceIdType.MESH)
    pl.semaphore_wait(barrier, chips + outer)

    for k in range(1, chips):
        copy_l(k).start()
    for k in [0] + hops:
        copy_y(k).start()
    later = [k for k in range(1, outer) if k not in hops]
    for k in later:
        copy_z(k).start()
    for k in [0] + hops:
        first = pl.multiple_of(from_z[k] * time, time)
        rec_all[:, pl.ds(first, time)] = rec[...] if k == 0 else near[hops.index(k)]

    half = round_up(-(-(sensors + 1) // 2), 16)
    inverse = covariance_inverse(
        unpack_halves(cross[:half, :]), sensors, count, 2, functools.partial(relay, later)
    )
    field = lead[...]
    for k in range(1, chips):
        copy_l(k).wait()
        field = field + got[k - 1]
    square = jnp.sum(jnp.sum(field * field, axis=0), axis=1, keepdims=True) / (3.0 * sensors)
    normed = field / jnp.sqrt(square + EPSILON)[None]
    solved = dot_full(normed.reshape(3 * own, mp), inverse).reshape(3, own, mp)
    gram = {}
    for c in range(3):
        for d in range(c, 3):
            gram[c, d] = jnp.sum(normed[c] * solved[d], axis=1, keepdims=True)
            gram[d, c] = gram[c, d]
    ridge = GRAM_RIDGE * (gram[0, 0] + gram[1, 1] + gram[2, 2]) / 3.0
    for c in range(3):
        gram[c, c] = gram[c, c] + ridge

    def cofactor(row, col):
        a, b, c, d = (row + 1) % 3, (row + 2) % 3, (col + 1) % 3, (col + 2) % 3
        return gram[a, c] * gram[b, d] - gram[a, d] * gram[b, c]

    determinant = gram[0, 0] * cofactor(0, 0) + gram[0, 1] * cofactor(0, 1) + gram[0, 2] * cofactor(0, 2)
    for c in range(3):
        mixed = sum((cofactor(d, c) / determinant) * solved[d] for d in range(3))
        filt[c, core] = mixed[:, :sensors].astype(BF16)
    copy_f.start()
    for k in range(outer):
        copy_y(k).wait()
    copy_f.wait()


def make_filters(inner, cross, lead, rec, near):
    nd, ns = lax.axis_size("node"), lax.axis_size("src")
    sensors, time = rec.shape
    own, mp = lead.shape[1:]
    outer = ns // inner
    vmem = pl.BlockSpec(memory_space=pltpu.VMEM)
    return pl.pallas_call(
        functools.partial(filter_kernel, nd, ns, inner, float(time * nd * ns)),
        out_shape=(
            jax.ShapeDtypeStruct((3, 2, own, sensors), BF16),
            jax.ShapeDtypeStruct((sensors, ns * time), BF16),
        ),
        in_specs=[vmem] * 4,
        out_specs=(vmem, vmem),
        scratch_shapes=[pltpu.VMEM((max(nd // 2 - 1, 1),) + lead.shape, F32)]
        + [pltpu.SemaphoreType.DMA((n,)) for n in (max(nd // 2 - 1, 1),) * 2 + (outer,) * 4]
        + [pltpu.SemaphoreType.DMA] * 2,
        compiler_params=pltpu.CompilerParams(collective_id=1, has_side_effects=True),
        name="filters",
    )(cross, lead, rec, near)


def local(transfer, node_pos, node_layer, layer_cond, tile_center, dip_tile, dip_offset, recording):
    sensors = transfer.shape[0]
    dipoles = dip_tile.shape[0]
    inner = math.gcd(lax.axis_size("src"), 2)
    cross, lead, near = lead_and_cross(
        inner, recording, transfer, node_pos, node_layer[None, :], layer_cond, tile_center, dip_tile[None, :], dip_offset
    )
    filters, samples = make_filters(inner, cross, lead, recording, near)
    out = jnp.dot(filters.reshape(3 * dipoles, sensors), samples, preferred_element_type=F32)
    return out.astype(BF16).reshape(3, dipoles, samples.shape[1])


def solution(mesh):
    return jax.shard_map(
        local,
        mesh=mesh,
        in_specs=(
            P(None, "node"),
            P(None, "node"),
            P("node"),
            P(),
            P(),
            P("src"),
            P(None, "src"),
            P(None, ("node", "src")),
        ),
        out_specs=P(None, "src", "node"),
        check_vma=False,
    )
```
